32 devices in a mesh: group: 4 (over z), local: 8 (over y, x, core).
Axes of the slice: x: 2, y: 2, z: 4, core: 2. Of those that a mesh axis runs over, the one named last changes fastest.
Arguments:
- tokens: bfloat16 [4096, 4096], P(('group', 'local')), may hold values from -6 to 6
- expert_ids: int32 [4096, 8], P(('group', 'local')), may hold values from 0 to 31, all different within a row; in each aligned block of 128 rows (0 to 127, 128 to 255, ...) at most 40 rows name the same one
- combine: float32 [4096, 8], P(('group', 'local')), may hold values from 0.02 to 0.5
- gate_w: bfloat16 [32, 4096, 768], P(('group', 'local')), may hold values from -0.09375 to 0.09375
- up_w: bfloat16 [32, 4096, 768], P(('group', 'local')), may hold values from -0.09375 to 0.09375
- down_w: bfloat16 [32, 768, 4096], P(('group', 'local')), may hold values from -0.21875 to 0.21875
Outputs:
- mixed: bfloat16 [4096, 4096], P(('group', 'local'))
The draws below stay inside these ranges and needn't reach their ends.
Inputs may be any that keep to these rules, and one draw needn't show every extreme that they name: `expert_ids`: each token names 8 different experts; among the 128 tokens of one device (aligned blocks) no expert is named more than 40 times, a bound that some block reaches.
All inputs are finite; a program needn't handle non-finite values.
Results may differ from the reference program's by a relative error of at most 0.0057.
Values may be sent and summed in bfloat16 or wider, within the bound.
A program may use at most 128 MiB of HBM per device.

```python
import math
import jax
import jax.numpy as jnp
import numpy as np
from jax import lax

D = 4096
FF = 768
TOP = 8
TOK_DEV = 128
EXPERTS = 32
CAP = 40
TOKENS = 4096
N_GROUP = 4
N_LOCAL = 8


def steps_of(rng, dims, shards, low, high):
    level = 1.0
    for dim, shards_of in shards:
        steps = jax.random.uniform(jax.random.fold_in(jax.random.fold_in(rng, 6), dim), (shards_of,), jnp.float32, low / len(shards), high / len(shards))
        level = level * jnp.repeat(jnp.exp(steps), dims[dim] // shards_of).reshape((-1,) + (1,) * (len(dims) - 1 - dim))
    return level


def deal_out(own_key, own, number, rows, count, top, bound, slope):
    order = jax.random.permutation(own_key, count)
    heavy_load, ordinary = load_shares(count, rows * top, bound, slope, True), load_shares(count, rows * top, bound, slope, False)
    places = jnp.arange(count)

    def named(sizes, offset_by):
        used = int((sizes > 0).sum())
        fixed = max(1, used // 4)
        passed = fixed + (places - fixed + offset_by * (used - fixed)) % max(1, count - fixed)
        return jnp.zeros((count,), jnp.int32).at[order[jnp.where(places < fixed, places, passed)]].set(jnp.asarray(sizes, jnp.int32))

    sizes = jnp.where(number % 4 == 0, named(heavy_load, number // 4), named(ordinary, number - number // 4 - 1))
    mixed = jax.random.permutation(jax.random.fold_in(own, 3), count)
    giver, taker = mixed[0:count // 2 * 2:2], mixed[1:count // 2 * 2:2]
    room = jnp.minimum(sizes[giver] - 1, bound - sizes[taker]) // 2
    room = jnp.where((giver == order[0]) | (taker == order[0]) | (sizes[taker] == 0), 0, jnp.maximum(room, 0))
    passed = jax.random.randint(jax.random.fold_in(own, 4), (count // 2,), 0, 1 << 20) % (room + 1)
    sizes = sizes.at[giver].add(-passed).at[taker].add(passed)
    labels = jnp.searchsorted(jnp.cumsum(sizes), jnp.arange(rows * top), side="right").astype(jnp.int32)
    listing = labels.reshape(top, rows).T
    listing = listing[jax.random.permutation(jax.random.fold_in(own, 1), rows)]
    offset_by = jax.random.randint(jax.random.fold_in(own, 2), (rows, 1), 0, top)
    return jnp.take_along_axis(listing, (jnp.arange(top)[None, :] + offset_by) % top, axis=1)


def load_shares(amount, total, most, lean, full):
    loads = [(1 << 20) // math.isqrt(rank ** lean) + 1 for rank in range(1, amount + 1)]
    largest = most if full else min(most, max(-(-total // amount), total * loads[0] // sum(loads)))
    least = 1 if total - largest >= amount - 1 else 0
    given, rest = [largest] + [least] * (amount - 1), total - largest - least * (amount - 1)
    while rest > 0:
        free = [i for i in range(1, amount) if given[i] < largest] or [i for i in range(1, amount) if given[i] < most]
        pool, budget = sum([loads[i] for i in free]), rest
        for i in free:
            more = min(most - given[i], max(1, budget * loads[i] // pool), rest)
            given[i] = given[i] + more
            rest = rest - more
    return np.array(given)


def normal_values(stream_key, dims, spread, bound, cuts=(), kind=jnp.bfloat16):
    loudness = steps_of(stream_key, dims, cuts, -0.22, 0.18) if cuts else 1.0
    values = jax.random.normal(stream_key, dims, jnp.float32) * spread * loudness
    return jnp.minimum(jnp.maximum(values, -bound), bound).astype(kind)


def setup_inputs(seed: int = 0) -> dict:
    streams_of = jax.random.split(jax.random.key(seed), 7)
    tokens = normal_values(streams_of[0], (TOKENS, D), 1.0, 6.0, ((0, 32),))
    expert_ids_keys = jax.random.split(jax.random.fold_in(streams_of[1], 1), TOKENS // TOK_DEV)
    expert_ids_turns = jax.random.permutation(jax.random.fold_in(streams_of[1], 3), TOKENS // TOK_DEV)
    expert_ids = jax.vmap(lambda own, number: deal_out(jax.random.fold_in(streams_of[1], 2), own, number, TOK_DEV, EXPERTS, TOP, CAP, 1))(expert_ids_keys, expert_ids_turns).reshape((TOKENS, TOP))
    combine = jnp.clip(jnp.exp(math.log(0.5) - 3.218876 * jax.random.uniform(streams_of[2], (TOKENS, TOP), jnp.float32) ** steps_of(streams_of[2], (TOKENS, TOP), ((0, 32),), -0.2, 0.2)), 0.02, 0.5)
    gate_w = normal_values(streams_of[3], (EXPERTS, D, FF), D ** -0.5, 0.09375, ((0, 32),))
    up_w = normal_values(streams_of[4], (EXPERTS, D, FF), D ** -0.5, 0.09375, ((0, 32),))
    down_w = normal_values(streams_of[5], (EXPERTS, FF, D), FF ** -0.5, 0.21875, ((0, 32),))
    return {"tokens": tokens, "expert_ids": expert_ids, "combine": combine, "gate_w": gate_w, "up_w": up_w, "down_w": down_w}


def reference(tokens, expert_ids, combine, gate_w, up_w, down_w):
    devices = N_GROUP * N_LOCAL
    flat_ids = expert_ids.reshape(devices, TOK_DEV * TOP).astype(jnp.int32)
    one_hot = (flat_ids[:, :, None] == jnp.arange(EXPERTS, dtype=jnp.int32)[None, None, :]).astype(jnp.int32)
    slot_index = jnp.sum((jnp.cumsum(one_hot, axis=1) - one_hot) * one_hot, axis=2).astype(jnp.int32)
    source = jnp.arange(devices, dtype=jnp.int32)[:, None]
    position = (flat_ids * (devices * CAP) + source * CAP + slot_index).reshape(-1)
    token_of = (jnp.arange(TOKENS * TOP, dtype=jnp.int32) // TOP).astype(jnp.int32)
    table = jnp.full((EXPERTS * devices * CAP,), TOKENS, jnp.int32).at[position].set(token_of)
    weight_table = jnp.zeros((EXPERTS * devices * CAP,), jnp.float32).at[position].set(combine.reshape(-1))
    padded = jnp.concatenate([tokens, jnp.zeros((1, D), tokens.dtype)], axis=0)

    def one_expert(total, inputs):
        gate_e, up_e, down_e, rows_e, weight_e = inputs
        chosen = padded[rows_e].astype(jnp.float32)
        gate_part = jnp.dot(chosen, gate_e.astype(jnp.float32), preferred_element_type=jnp.float32)
        up_part = jnp.dot(chosen, up_e.astype(jnp.float32), preferred_element_type=jnp.float32)
        hidden = (jax.nn.silu(gate_part) * up_part).astype(jnp.bfloat16)
        result = jnp.dot(hidden.astype(jnp.float32), down_e.astype(jnp.float32), preferred_element_type=jnp.float32).astype(jnp.bfloat16)
        total = total.at[rows_e].add(weight_e[:, None] * result.astype(jnp.float32))
        return total, None

    start = jnp.zeros((TOKENS + 1, D), jnp.float32)
    total, _ = lax.scan(one_expert, start, (gate_w, up_w, down_w, table.reshape(EXPERTS, devices * CAP), weight_table.reshape(EXPERTS, devices * CAP)))
    return total[:TOKENS].astype(jnp.bfloat16)
```

```python
import functools

import jax
import jax.numpy as jnp
from jax import lax
from jax.experimental import pallas as pl
from jax.experimental.pallas import tpu as pltpu
from jax.sharding import PartitionSpec as P

MESH = pl.DeviceIdType.MESH


def routing(expert_ids, combine, experts):
    rows = expert_ids.shape[0]
    named = expert_ids.T[:, None, :] == jnp.arange(experts, dtype=jnp.int32)[None, :, None]
    member = jnp.sum(named.astype(jnp.float32), axis=0)
    weight = jnp.sum(jnp.where(named, combine.T[:, None, :], 0.0), axis=0)
    before = (jnp.arange(rows)[:, None] < jnp.arange(rows)[None, :]).astype(jnp.bfloat16)
    rank = jnp.dot(member.astype(jnp.bfloat16), before, preferred_element_type=jnp.float32)
    return jnp.where(member > 0, rank, -1.0), weight


def plain(tokens, expert_ids, combine, gate_w, up_w, down_w):
    rows, features = tokens.shape
    groups = lax.axis_size("group")
    members = lax.axis_size("local")
    experts = groups * members
    capacity = max(2, rows * expert_ids.shape[1] * 5 // (4 * experts))
    slot, weight = routing(expert_ids, combine, experts)
    table = jnp.stack([slot, weight]).reshape(2, groups, members, rows)
    table = lax.all_to_all(table, "group", split_axis=1, concat_axis=1, tiled=True)
    slot, weight = table[0], table[1]
    blocks = lax.all_gather(tokens, "group")
    picks = slot[:, :, None, :] == jnp.arange(capacity, dtype=jnp.float32)[None, None, :, None]
    chosen = jnp.einsum(
        "blct,btd->blcd", picks.astype(jnp.bfloat16), blocks, preferred_element_type=jnp.float32
    ).astype(jnp.bfloat16)
    arrived = lax.all_to_all(chosen, "local", split_axis=1, concat_axis=1, tiled=True)
    x = arrived.reshape(-1, features)
    gate_part = jnp.dot(x, gate_w[0], preferred_element_type=jnp.float32)
    up_part = jnp.dot(x, up_w[0], preferred_element_type=jnp.float32)
    hidden = (jax.nn.silu(gate_part) * up_part).astype(jnp.bfloat16)
    result = jnp.dot(hidden, down_w[0], preferred_element_type=jnp.float32).astype(jnp.bfloat16)
    returned = lax.all_to_all(
        result.reshape(arrived.shape), "local", split_axis=1, concat_axis=1, tiled=True
    ).reshape(groups, members * capacity, features)
    mix = jnp.where(picks, weight[:, :, None, :], 0.0).reshape(groups, members * capacity, rows)
    high = mix.astype(jnp.bfloat16)
    low = (mix - high.astype(jnp.float32)).astype(jnp.bfloat16)
    part = jnp.einsum("bct,bcd->btd", high, returned, preferred_element_type=jnp.float32)
    part = part + jnp.einsum("bct,bcd->btd", low, returned, preferred_element_type=jnp.float32)
    return lax.psum_scatter(part.astype(jnp.bfloat16), "group", scatter_dimension=0, tiled=False)


def layer(capacity, tokens, table, gate_w, up_w, down_w, out,
          block, routes, sending, rows, back, gate, up, down, hidden, mix, parts, chain, total,
          load_sem, t_send, t_recv, z_send, z_recv, a_send, a_recv,
          x_send, x_recv, r_send, r_recv, e_send, e_recv, p_send, p_recv):
    groups, members = 4, 8
    g = lax.axis_index("group")
    me = lax.axis_index("local")
    at_y, at_x, at_c = me // 4, lax.rem(me // 2, 2), lax.rem(me, 2)
    count, features = tokens.shape
    piece_rows = 2 * capacity
    width = 4 * piece_rows
    half = features // 2
    wide = 512
    tiles = features // wide
    half_tiles = tiles // 2

    def group_at(j):
        return lax.rem(g + j, groups)

    def at(y, x, c):
        return 4 * lax.rem(at_y + y, 2) + 2 * lax.rem(at_x + x, 2) + lax.rem(at_c + c, 2)

    def first(h):
        return at(h, 1 - h, 0)

    def partner(h, p):
        second = p // 2
        return at(second * (1 - h), second * h, lax.rem(p, 2))

    def cols_of(h):
        return pl.ds(pl.multiple_of(h * half, half), half)

    def tile(n):
        return pl.ds(pl.multiple_of(n * wide, wide), wide)

    def piece(p):
        return pl.ds(pl.multiple_of(p * piece_rows, 16), piece_rows)

    own, near = pl.ds(0, count), pl.ds(count, count)

    def remote(src, dst, send, recv, group, local):
        return pltpu.make_async_remote_copy(
            src_ref=src, dst_ref=dst, send_sem=send, recv_sem=recv,
            device_id=(group, local), device_id_type=MESH)

    def t_copy(j, r):
        to = group_at(groups - j)
        return remote(table.at[to], routes.at[j, r], t_send.at[j, r], t_recv.at[j, r],
                      to, me if r == 0 else first(r - 1))

    def z_copy(j):
        return remote(block.at[j - 1, own], block.at[j, own], z_send.at[j], z_recv.at[j],
                      group_at(groups - 1), me)

    def a_copy(j, h):
        return remote(block.at[j, own, cols_of(h)], block.at[j, near, cols_of(h)],
                      a_send.at[j, h], a_recv.at[j, h], g, first(h))

    def x_copy(j, h, p):
        return remote(sending.at[lax.min(j, 1), piece(p - 1), cols_of(h)], rows.at[j, piece(p), cols_of(h)],
                      x_send.at[j, h, p], x_recv.at[j, h, p], g, partner(h, p))

    def r_copy(j, n, p):
        return remote(rows.at[j, piece(p), tile(n)], back.at[j, piece(p), tile(n)],
                      r_send.at[j, n, p], r_recv.at[j, n, p], g, partner(n // half_tiles, p))

    def e_copy(j, n):
        return remote(block.at[j, near, tile(n)], parts.at[j, :, tile(n)],
                      e_send.at[j, n], e_recv.at[j, n], g, first(n // half_tiles))

    def p_copy(j, n):
        return remote(block.at[j, own, tile(n)], chain.at[j - 1, :, tile(n)],
                      p_send.at[j, n], p_recv.at[j, n], group_at(groups - 1), me)

    loads = [
        pltpu.make_async_copy(tokens, block.at[0, own], load_sem.at[0]),
        pltpu.make_async_copy(gate_w, gate, load_sem.at[1]),
        pltpu.make_async_copy(up_w, up, load_sem.at[2]),
        pltpu.make_async_copy(down_w, down, load_sem.at[3]),
    ]
    loads[0].start()
    routes[0, 0] = table[g]
    barrier = pltpu.get_barrier_semaphore()
    peers = [(g, partner(h, p)) for h in range(2) for p in (1, 2, 3) if (h, p) != (1, 1)]
    peers += [(group_at(j), to) for j in range(1, groups) for to in (me, first(0), first(1))]
    for peer in peers:
        pl.semaphore_signal(barrier, inc=1, device_id=peer, device_id_type=MESH)
    pl.semaphore_wait(barrier, len(peers))
    for j in range(groups):
        for r in range(3):
            if (j, r) != (0, 0):
                t_copy(j, r).start()
    loads[0].wait()

    def begin(j):
        @pl.when(j >= 1)
        def _():
            z_copy(j).wait()

        @pl.when(j + 1 < groups)
        def _():
            z_copy(j + 1).start()

        for h in range(2):
            a_copy(j, h).start()

    def slots_of(j, h):
        lanes = []
        for p in range(4):
            e = partner(h, p)
            near_slot = routes[j, 1 + h, pl.ds(e, 1), :] + float(capacity)
            lanes.append(jnp.concatenate([routes[j, 0, pl.ds(e, 1), :], near_slot], axis=1))
        return lanes

    def weights_of(j, h):
        lanes = []
        for p in range(4):
            e = members + partner(h, p)
            lanes.append(jnp.concatenate(
                [routes[j, 0, pl.ds(e, 1), :], routes[j, 1 + h, pl.ds(e, 1), :]], axis=1))
        return lanes

    def places():
        return lax.broadcasted_iota(jnp.int32, (piece_rows, 2 * count), 0).astype(jnp.float32)

    def dispatch(j):
        for r in range(3):
            if r == 0:
                @pl.when(j >= 1)
                def _():
                    t_copy(j, 0).wait()
            else:
                t_copy(j, r).wait()
        for h in range(2):
            a_copy(j, h).wait()
            picks = jnp.concatenate(
                [jnp.where(slot == places(), 1.0, 0.0) for slot in slots_of(j, h)], axis=0
            ).astype(jnp.bfloat16)

            @pl.loop(h * half_tiles, (h + 1) * half_tiles)
            def _(n):
                chosen = jnp.dot(
                    picks, block[j, :, tile(n)], preferred_element_type=jnp.float32
                ).astype(jnp.bfloat16)
                rows[j, 0:piece_rows, tile(n)] = chosen[0:piece_rows]
                sending[lax.min(j, 1), :, tile(n)] = chosen[piece_rows:width]

            for p in (2, 3, 1):
                x_copy(j, h, p).start()

    def swapped(v):
        groups_of = [v[k * capacity : (k + 1) * capacity] for k in range(8)]
        return jnp.concatenate(
            [groups_of[4 * k + 2 * c + s] for s in range(2) for c in range(2) for k in range(2)], axis=0)

    def compute(j):
        @pl.when(j == 1)
        def _():
            loads[1].wait()
            loads[2].wait()
            loads[3].wait()

        for h in range(2):
            for p in (1, 2, 3):
                x_copy(j, h, p).wait()

        units = hidden.shape[2]

        @pl.loop(0, units // 256)
        def _(n):
            cols = pl.ds(pl.multiple_of(n * 256, 256), 256)

            def project(bank):
                left = jnp.dot(rows[j, :, 0:half], bank[0:half, cols], preferred_element_type=jnp.float32)
                right = jnp.dot(rows[j, :, half:features], bank[half:features, cols],
                                preferred_element_type=jnp.float32)
                return left + swapped(right)

            a = project(gate)
            b = project(up)
            value = jax.nn.silu(a) * b
            hidden[0, :, cols] = value.astype(jnp.bfloat16)
            hidden[1, :, cols] = swapped(value).astype(jnp.bfloat16)

        @pl.loop(0, tiles)
        def _(n):
            result = jnp.dot(
                hidden[n // half_tiles], down[:, tile(n)], preferred_element_type=jnp.float32
            ).astype(jnp.bfloat16)
            back[j, 0:piece_rows, tile(n)] = result[0:piece_rows]
            rows[j, piece_rows:width, tile(n)] = result[piece_rows:width]
            for p in (2, 3, 1):
                r_copy(j, n, p).start()

    def gather(j):
        unit = jnp.where(
            lax.broadcasted_iota(jnp.int32, (2 * count, 2 * count), 0)
            == lax.broadcasted_iota(jnp.int32, (2 * count, 2 * count), 1), 1.0, 0.0).astype(jnp.bfloat16)
        for h in range(2):
            weights = jnp.concatenate(
                [jnp.where(slot == places(), weight, 0.0)
                 for slot, weight in zip(slots_of(j, h), weights_of(j, h))], axis=0)
            mix[h] = lax.dot_general(
                unit, weights.astype(jnp.bfloat16), (((1,), (1,)), ((), ())),
                preferred_element_type=jnp.float32).astype(jnp.bfloat16)

        @pl.loop(0, tiles)
        def _(n):
            for p in (1, 2, 3):
                r_copy(j, n, p).wait()
            both = jnp.dot(mix[n // half_tiles], back[j, :, tile(n)], preferred_element_type=jnp.float32)
            block[j, near, tile(n)] = both[count : 2 * count].astype(jnp.bfloat16)
            e_copy(j, n).start()
            total[:, tile(n)] = both[0:count]

    def finish(j):
        @pl.loop(0, tiles)
        def _(n):
            e_copy(j, n).wait()
            part = total[:, tile(n)] + parts[j, :, tile(n)].astype(jnp.float32)

            @pl.when(j == 1)
            def _():
                block[j, own, tile(n)] = part.astype(jnp.bfloat16)

            @pl.when(j >= 2)
            def _():
                p_copy(j - 1, n).wait()
                block[j, own, tile(n)] = (
                    part + chain[j - 2, :, tile(n)].astype(jnp.float32)).astype(jnp.bfloat16)

            p_copy(j, n).start()

    @pl.loop(0, 2 * groups - 1)
    def _(step):
        @pl.when(step < groups)
        def _():
            begin(step)

        @pl.when(step == 0)
        def _():
            for load in loads[1:]:
                load.start()

        @pl.when(step >= groups)
        def _():
            gather(step - groups + 1)

        @pl.when((step >= 2) & (step < groups + 2))
        def _():
            compute(lax.rem(step - 1, groups))

        @pl.when(step < groups)
        def _():
            dispatch(step)

        @pl.when(step >= groups)
        def _():
            finish(step - groups + 1)

    gather(0)

    @pl.loop(0, tiles)
    def _(n):
        e_copy(0, n).wait()
        p_copy(groups - 1, n).wait()
        out[:, tile(n)] = (
            total[:, tile(n)] + parts[0, :, tile(n)].astype(jnp.float32)
            + chain[groups - 2, :, tile(n)].astype(jnp.float32)).astype(jnp.bfloat16)


def fused(tokens, expert_ids, combine, gate_w, up_w, down_w):
    count, features = tokens.shape
    units = gate_w.shape[2]
    groups = lax.axis_size("group")
    members = lax.axis_size("local")
    experts = groups * members
    capacity = max(2, count * expert_ids.shape[1] * 5 // (4 * experts))
    if (groups, members) != (4, 8) or capacity % 8 or features % 1024 or units % 256 or count % 128:
        return plain(tokens, expert_ids, combine, gate_w, up_w, down_w)
    slot, weight = routing(expert_ids, combine, experts)
    slot = jnp.where(slot < 0, -1.0 - capacity, slot)
    table = jnp.concatenate(
        [slot.reshape(groups, members, count), weight.reshape(groups, members, count)], axis=1)
    width = members * capacity
    tiles = features // 512
    half = jnp.bfloat16
    dma = pltpu.SemaphoreType.DMA
    anywhere = pl.BlockSpec(memory_space=pl.ANY)
    inside = pl.BlockSpec(memory_space=pltpu.VMEM)
    return pl.pallas_call(
        functools.partial(layer, capacity),
        out_shape=jax.ShapeDtypeStruct((count, features), half),
        in_specs=[anywhere, inside, anywhere, anywhere, anywhere],
        out_specs=inside,
        scratch_shapes=[
            pltpu.VMEM((groups, 2 * count, features), half),
            pltpu.VMEM((groups, 3, 2 * members, count), jnp.float32),
            pltpu.VMEM((2, width * 3 // 4, features), half),
            pltpu.VMEM((groups, width, features), half),
            pltpu.VMEM((groups, width, features), half),
            pltpu.VMEM((features, units), half),
            pltpu.VMEM((features, units), half),
            pltpu.VMEM((units, features), half),
            pltpu.VMEM((2, width, units), half),
            pltpu.VMEM((2, 2 * count, width), half),
            pltpu.VMEM((groups, count, features), half),
            pltpu.VMEM((groups - 1, count, features), half),
            pltpu.VMEM((count, features), jnp.float32),
            dma((4,)),
            dma((groups, 3)), dma((groups, 3)),
            dma((groups,)), dma((groups,)),
            dma((groups, 2)), dma((groups, 2)),
            dma((groups, 2, 4)), dma((groups, 2, 4)),
            dma((groups, tiles, 4)), dma((groups, tiles, 4)),
            dma((groups, tiles)), dma((groups, tiles)),
            dma((groups, tiles)), dma((groups, tiles)),
        ],
        compiler_params=pltpu.CompilerParams(
            collective_id=0, has_side_effects=True, vmem_limit_bytes=62 * 1024 * 1024),
    )(tokens, table, gate_w[0], up_w[0], down_w[0])


def solution(mesh):
    rows = P(("group", "local"), None)
    banks = P(("group", "local"), None, None)
    return jax.shard_map(
        fused,
        mesh=mesh,
        in_specs=(rows, rows, rows, banks, banks, banks),
        out_specs=rows,
        check_vma=False,
    )
```

```python
import functools

import jax
import jax.numpy as jnp
from jax import lax
from jax.experimental import pallas as pl
from jax.experimental.pallas import tpu as pltpu
from jax.sharding import PartitionSpec as P

MESH = pl.DeviceIdType.MESH


def routing(expert_ids, combine, experts):
    rows = expert_ids.shape[0]
    named = expert_ids.T[:, None, :] == jnp.arange(experts, dtype=jnp.int32)[None, :, None]
    member = jnp.sum(named.astype(jnp.float32), axis=0)
    weight = jnp.sum(jnp.where(named, combine.T[:, None, :], 0.0), axis=0)
    before = (jnp.arange(rows)[:, None] < jnp.arange(rows)[None, :]).astype(jnp.bfloat16)
    rank = jnp.dot(member.astype(jnp.bfloat16), before, preferred_element_type=jnp.float32)
    return jnp.where(member > 0, rank, -1.0), weight


def plain(tokens, expert_ids, combine, gate_w, up_w, down_w):
    rows, features = tokens.shape
    groups = lax.axis_size("group")
    members = lax.axis_size("local")
    experts = groups * members
    capacity = max(2, rows * expert_ids.shape[1] * 5 // (4 * experts))
    slot, weight = routing(expert_ids, combine, experts)
    table = jnp.stack([slot, weight]).reshape(2, groups, members, rows)
    table = lax.all_to_all(table, "group", split_axis=1, concat_axis=1, tiled=True)
    slot, weight = table[0], table[1]
    blocks = lax.all_gather(tokens, "group")
    picks = slot[:, :, None, :] == jnp.arange(capacity, dtype=jnp.float32)[None, None, :, None]
    chosen = jnp.einsum(
        "blct,btd->blcd", picks.astype(jnp.bfloat16), blocks, preferred_element_type=jnp.float32
    ).astype(jnp.bfloat16)
    arrived = lax.all_to_all(chosen, "local", split_axis=1, concat_axis=1, tiled=True)
    x = arrived.reshape(-1, features)
    gate_part = jnp.dot(x, gate_w[0], preferred_element_type=jnp.float32)
    up_part = jnp.dot(x, up_w[0], preferred_element_type=jnp.float32)
    hidden = (jax.nn.silu(gate_part) * up_part).astype(jnp.bfloat16)
    result = jnp.dot(hidden, down_w[0], preferred_element_type=jnp.float32).astype(jnp.bfloat16)
    returned = lax.all_to_all(
        result.reshape(arrived.shape), "local", split_axis=1, concat_axis=1, tiled=True
    ).reshape(groups, members * capacity, features)
    mix = jnp.where(picks, weight[:, :, None, :], 0.0).reshape(groups, members * capacity, rows)
    high = mix.astype(jnp.bfloat16)
    low = (mix - high.astype(jnp.float32)).astype(jnp.bfloat16)
    part = jnp.einsum("bct,bcd->btd", high, returned, preferred_element_type=jnp.float32)
    part = part + jnp.einsum("bct,bcd->btd", low, returned, preferred_element_type=jnp.float32)
    return lax.psum_scatter(part.astype(jnp.bfloat16), "group", scatter_dimension=0, tiled=False)


def layer(capacity, lead, ids, combine, tokens, gate_w, up_w, down_w, out,
          block, tables, near_tables, picks, sending, rows, back, gate, up, down, hidden, mix,
          parts, lead_parts, chain, lead_chain, total,
          load_sem, t_send, t_recv, n_send, n_recv, z_send, z_recv, a_send, a_recv,
          x_send, x_recv, r_send, r_recv, e_send, e_recv, p_send, p_recv):
    groups, members = 4, 8
    g = lax.axis_index("group")
    me = lax.axis_index("local")
    at_y, at_x, at_c = me // 4, lax.rem(me // 2, 2), lax.rem(me, 2)
    count, features = tokens.shape
    experts = groups * members
    piece_rows = 2 * capacity
    width = 4 * piece_rows
    half = features // 2
    wide = 512
    half_tiles = (half - lead) // wide
    tiles = 2 * half_tiles
    f32, bf16 = jnp.float32, jnp.bfloat16

    def group_at(j):
        return lax.rem(g + j, groups)

    def at(y, x, c):
        return 4 * lax.rem(at_y + y, 2) + 2 * lax.rem(at_x + x, 2) + lax.rem(at_c + c, 2)

    def first(h):
        return at(h, 1 - h, 0)

    def partner(h, p):
        second = p // 2
        return at(second * (1 - h), second * h, lax.rem(p, 2))

    starts = (0, lead, half, features - lead)
    sizes = (lead, half - lead, half - lead, lead)

    def span(u):
        return pl.ds(starts[u], sizes[u])

    def tile(n):
        return pl.ds(pl.multiple_of(lead + n * wide, 128), wide)

    def packed(n):
        return pl.ds(pl.multiple_of(n * wide, 128), wide)

    def piece(p):
        return pl.ds(pl.multiple_of(p * piece_rows, 16), piece_rows)

    own, near, pair = pl.ds(0, count), pl.ds(count, count), pl.ds(0, 2 * count)

    def remote(src, dst, send, recv, group, local):
        return pltpu.make_async_remote_copy(
            src_ref=src, dst_ref=dst, send_sem=send, recv_sem=recv,
            device_id=(group, local), device_id_type=MESH)

    before_me = group_at(groups - 1)

    def t_copy(j):
        return remote(tables.at[j - 1], tables.at[j], t_send.at[j], t_recv.at[j], before_me, me)

    def n_copy(j, h):
        return remote(tables.at[j, g], near_tables.at[j, h], n_send.at[j, h], n_recv.at[j, h],
                      g, first(h))

    def z_copy(j, u):
        which = own if u in (1, 2) else pair
        return remote(block.at[j - 1, which, span(u)], block.at[j, which, span(u)],
                      z_send.at[j, u], z_recv.at[j, u], before_me, me)

    def a_copy(j, u):
        return remote(block.at[j, own, span(u)], block.at[j, near, span(u)],
                      a_send.at[j, u], a_recv.at[j, u], g, first(u // 2))

    def x_copy(j, u, p):
        return remote(sending.at[lax.min(j, 1), piece(p - 1), span(u)], rows.at[j, piece(p), span(u)],
                      x_send.at[j, u, p], x_recv.at[j, u, p], g, partner(u // 2, p))

    def wide_tile(n):
        return tile(n), n // half_tiles, n

    def lead_tile(h):
        return span(3 * h), h, tiles + h

    def r_copy(j, of, p):
        cols, h, n = of
        return remote(rows.at[j, piece(p), cols], back.at[j, piece(p), cols],
                      r_send.at[j, n, p], r_recv.at[j, n, p], g, partner(h, p))

    def e_copy(j, of):
        cols, h, n = of
        landing = lead_parts.at[h] if isinstance(h, int) else parts.at[j, :, packed(n)]
        return remote(block.at[j, near, cols], landing,
                      e_send.at[j, n], e_recv.at[j, n], g, first(h))

    def p_copy(j, n):
        return remote(block.at[j, own, tile(n)], chain.at[j - 1, :, packed(n)],
                      p_send.at[j, n], p_recv.at[j, n], before_me, me)

    def q_copy(j, h):
        return remote(block.at[j, pair, span(3 * h)], lead_chain.at[j - 1, h],
                      p_send.at[j, tiles + h], p_recv.at[j, tiles + h], before_me, me)

    loads = [
        pltpu.make_async_copy(tokens, block.at[0, own], load_sem.at[0]),
        pltpu.make_async_copy(gate_w, gate, load_sem.at[1]),
        pltpu.make_async_copy(up_w, up, load_sem.at[2]),
        pltpu.make_async_copy(down_w, down, load_sem.at[3]),
    ]
    loads[0].start()
    barrier = pltpu.get_barrier_semaphore()
    peers = [(g, partner(h, p)) for h in range(2) for p in (1, 2, 3) if (h, p) != (1, 1)]
    peers += [(group_at(1), me), (before_me, me)]
    for peer in peers:
        pl.semaphore_signal(barrier, inc=1, device_id=peer, device_id_type=MESH)

    def iota(shape, axis):
        return lax.broadcasted_iota(jnp.int32, shape, axis)

    member = jnp.zeros((experts, count), f32)
    weight = jnp.zeros((experts, count), f32)
    for k in range(ids.shape[0]):
        named = ids[k : k + 1, :] == iota((experts, count), 0)
        member = member + jnp.where(named, 1.0, 0.0)
        weight = weight + jnp.where(named, combine[k : k + 1, :], 0.0)
    before = jnp.where(iota((count, count), 0) < iota((count, count), 1), 1.0, 0.0).astype(bf16)
    rank = jnp.dot(member.astype(bf16), before, preferred_element_type=f32)
    slot = jnp.where(member > 0, rank, -1.0 - capacity)
    for q in range(groups):
        tables[0, q, 0:members] = slot[q * members : (q + 1) * members]
        tables[0, q, members : 2 * members] = weight[q * members : (q + 1) * members]

    pl.semaphore_wait(barrier, len(peers))
    loads[0].wait()

    def slots_of(j, h):
        lanes = []
        for p in range(4):
            e = partner(h, p)
            near_slot = near_tables[j, h, pl.ds(e, 1), :] + float(capacity)
            lanes.append(jnp.concatenate([tables[j, g, pl.ds(e, 1), :], near_slot], axis=1))
        return lanes

    def weights_of(j, h):
        lanes = []
        for p in range(4):
            e = members + partner(h, p)
            lanes.append(jnp.concatenate(
                [tables[j, g, pl.ds(e, 1), :], near_tables[j, h, pl.ds(e, 1), :]], axis=1))
        return lanes

    def places():
        return iota((piece_rows, 2 * count), 0).astype(f32)

    def begin(j):
        @pl.when(j >= 1)
        def _():
            t_copy(j).wait()

        for h in range(2):
            n_copy(j, h).start()

        @pl.when(j + 1 < groups)
        def _():
            t_copy(j + 1).start()

        @pl.when(j == 0)
        def _():
            for u in (0, 3):
                a_copy(j, u).start()

        for u in (1, 2):
            @pl.when(j >= 1)
            def _():
                z_copy(j, u).wait()

            a_copy(j, u).start()

            @pl.when(j + 1 < groups)
            def _():
                z_copy(j + 1, u).start()

    def pick(j, u):
        h = u // 2

        def choose(cols):
            chosen = jnp.dot(
                picks[h], block[j, :, cols], preferred_element_type=f32).astype(bf16)
            rows[j, 0:piece_rows, cols] = chosen[0:piece_rows]
            sending[lax.min(j, 1), :, cols] = chosen[piece_rows:width]

        if u in (1, 2):
            @pl.loop(h * half_tiles, (h + 1) * half_tiles)
            def _(n):
                choose(tile(n))
        else:
            choose(span(u))
        for p in (2, 3, 1):
            x_copy(j, u, p).start()

    def prepare(j):
        for h in range(2):
            n_copy(j, h).wait()
            picks[h] = jnp.concatenate(
                [jnp.where(slot == places(), 1.0, 0.0) for slot in slots_of(j, h)], axis=0
            ).astype(bf16)

    def dispatch(j):
        prepare(j)

        def leads():
            for u in (0, 3):
                @pl.when(j == 0)
                def _():
                    a_copy(j, u).wait()

                @pl.when(j >= 1)
                def _():
                    z_copy(j, u).wait()

                @pl.when(j + 1 < groups)
                def _():
                    z_copy(j + 1, u).start()
            for u in (0, 3):
                pick(j, u)

        @pl.when(j == 0)
        def _():
            leads()

        for u in (1, 2):
            a_copy(j, u).wait()
            pick(j, u)

        @pl.when(j >= 1)
        def _():
            leads()

    def swapped(v):
        groups_of = [v[k * capacity : (k + 1) * capacity] for k in range(8)]
        return jnp.concatenate(
            [groups_of[4 * k + 2 * c + s] for s in range(2) for c in range(2) for k in range(2)], axis=0)

    def compute(j):
        @pl.when(j == 1)
        def _():
            loads[1].wait()
            loads[2].wait()
            loads[3].wait()

        for u in range(4):
            for p in (1, 2, 3):
                x_copy(j, u, p).wait()

        units = hidden.shape[2]

        @pl.loop(0, units // 256)
        def _(n):
            cols = pl.ds(pl.multiple_of(n * 256, 256), 256)

            def project(bank):
                left = jnp.dot(rows[j, :, 0:half], bank[0:half, cols], preferred_element_type=f32)
                right = jnp.dot(rows[j, :, half:features], bank[half:features, cols],
                                preferred_element_type=f32)
                return left + swapped(right)

            a = project(gate)
            b = project(up)
            value = jax.nn.silu(a) * b
            hidden[0, :, cols] = value.astype(bf16)
            hidden[1, :, cols] = swapped(value).astype(bf16)

        def project_back(of):
            cols, h, _ = of
            result = jnp.dot(hidden[h], down[:, cols], preferred_element_type=f32).astype(bf16)
            back[j, 0:piece_rows, cols] = result[0:piece_rows]
            rows[j, piece_rows:width, cols] = result[piece_rows:width]
            for p in (2, 3, 1):
                r_copy(j, of, p).start()

        for h in range(2):
            project_back(lead_tile(h))

        @pl.loop(0, tiles)
        def _(n):
            project_back(wide_tile(n))

    def gather(j, last):
        unit = jnp.where(iota((2 * count, 2 * count), 0) == iota((2 * count, 2 * count), 1), 1.0, 0.0).astype(bf16)
        for h in range(2):
            weights = jnp.concatenate(
                [jnp.where(slot == places(), weight, 0.0)
                 for slot, weight in zip(slots_of(j, h), weights_of(j, h))], axis=0)
            mix[h] = lax.dot_general(
                unit, weights.astype(bf16), (((1,), (1,)), ((), ())),
                preferred_element_type=f32).astype(bf16)

        def mixed(of):
            cols, h, _ = of
            for p in (1, 2, 3):
                r_copy(j, of, p).wait()
            return jnp.dot(mix[h], back[j, :, cols], preferred_element_type=f32)

        for h in range(2):
            of = lead_tile(h)
            both = mixed(of)
            if last:
                q_copy(groups - 1, h).wait()
                both = both + lead_chain[groups - 2, h].astype(f32)
                block[j, near, of[0]] = both[count : 2 * count].astype(bf16)
                e_copy(j, of).start()
                total[:, of[0]] = both[0:count]
            else:
                @pl.when(j == 1)
                def _():
                    block[j, :, of[0]] = both.astype(bf16)

                @pl.when(j >= 2)
                def _():
                    q_copy(j - 1, h).wait()
                    block[j, :, of[0]] = (both + lead_chain[j - 2, h].astype(f32)).astype(bf16)

                q_copy(j, h).start()

        @pl.loop(0, tiles)
        def _(n):
            of = wide_tile(n)
            both = mixed(of)
            block[j, near, of[0]] = both[count : 2 * count].astype(bf16)
            e_copy(j, of).start()
            total[:, of[0]] = both[0:count]

    def arrived(j, n):
        return chain[j, :, packed(n)].astype(f32)

    def finish(j):
        @pl.loop(0, tiles)
        def _(n):
            e_copy(j, wide_tile(n)).wait()
            part = total[:, tile(n)] + parts[j, :, packed(n)].astype(f32)

            @pl.when(j == 1)
            def _():
                block[j, own, tile(n)] = part.astype(bf16)

            @pl.when(j >= 2)
            def _():
                p_copy(j - 1, n).wait()
                block[j, own, tile(n)] = (part + arrived(j - 2, n)).astype(bf16)

            p_copy(j, n).start()

    @pl.loop(0, 2 * groups - 1)
    def _(step):
        @pl.when(step < groups)
        def _():
            begin(step)

        @pl.when(step == 0)
        def _():
            for load in loads[1:]:
                load.start()

        @pl.when(step >= groups)
        def _():
            gather(step - groups + 1, False)

        @pl.when((step >= 2) & (step < groups + 2))
        def _():
            compute(lax.rem(step - 1, groups))

        @pl.when(step < groups)
        def _():
            dispatch(step)

        @pl.when(step >= groups)
        def _():
            finish(step - groups + 1)

    gather(0, True)
    for h in range(2):
        cols = lead_tile(h)[0]
        e_copy(0, lead_tile(h)).wait()
        out[:, cols] = (total[:, cols] + lead_parts[h].astype(f32)).astype(bf16)

    @pl.loop(0, tiles)
    def _(n):
        e_copy(0, wide_tile(n)).wait()
        p_copy(groups - 1, n).wait()
        out[:, tile(n)] = (
            total[:, tile(n)] + parts[0, :, packed(n)].astype(f32) + arrived(groups - 2, n)).astype(bf16)


def fused(tokens, expert_ids, combine, gate_w, up_w, down_w):
    count, features = tokens.shape
    units = gate_w.shape[2]
    groups = lax.axis_size("group")
    members = lax.axis_size("local")
    experts = groups * members
    capacity = max(2, count * expert_ids.shape[1] * 5 // (4 * experts))
    if (groups, members) != (4, 8) or capacity % 8 or features % 2048 or units % 256 or count % 128:
        return plain(tokens, expert_ids, combine, gate_w, up_w, down_w)
    width = members * capacity
    lead = features // 8
    slots = 2 * ((features // 2 - lead) // 512) + 2
    half = jnp.bfloat16
    dma = pltpu.SemaphoreType.DMA
    anywhere = pl.BlockSpec(memory_space=pl.ANY)
    inside = pl.BlockSpec(memory_space=pltpu.VMEM)
    return pl.pallas_call(
        functools.partial(layer, capacity, lead),
        out_shape=jax.ShapeDtypeStruct((count, features), half),
        in_specs=[inside, inside, anywhere, anywhere, anywhere, anywhere],
        out_specs=inside,
        scratch_shapes=[
            pltpu.VMEM((groups, 2 * count, features), half),
            pltpu.VMEM((groups, groups, 2 * members, count), jnp.float32),
            pltpu.VMEM((groups, 2, 2 * members, count), jnp.float32),
            pltpu.VMEM((2, width, 2 * count), half),
            pltpu.VMEM((2, width * 3 // 4, features), half),
            pltpu.VMEM((groups, width, features), half),
            pltpu.VMEM((groups, width, features), half),
            pltpu.VMEM((features, units), half),
            pltpu.VMEM((features, units), half),
            pltpu.VMEM((units, features), half),
            pltpu.VMEM((2, width, units), half),
            pltpu.VMEM((2, 2 * count, width), half),
            pltpu.VMEM((groups, count, features - 2 * lead), half),
            pltpu.VMEM((2, count, lead), half),
            pltpu.VMEM((groups - 1, count, features - 2 * lead), half),
            pltpu.VMEM((groups - 1, 2, 2 * count, lead), half),
            pltpu.VMEM((count, features), jnp.float32),
            dma((4,)),
            dma((groups,)), dma((groups,)),
            dma((groups, 2)), dma((groups, 2)),
            dma((groups, 4)), dma((groups, 4)),
            dma((groups, 4)), dma((groups, 4)),
            dma((groups, 4, 4)), dma((groups, 4, 4)),
            dma((groups, slots, 4)), dma((groups, slots, 4)),
            dma((groups, slots)), dma((groups, slots)),
            dma((groups, slots)), dma((groups, slots)),
        ],
        compiler_params=pltpu.CompilerParams(
            collective_id=0, has_side_effects=True, vmem_limit_bytes=63 * 1024 * 1024),
    )(expert_ids.T, combine.T, tokens, gate_w[0], up_w[0], down_w[0])


def solution(mesh):
    rows = P(("group", "local"), None)
    banks = P(("group", "local"), None, None)
    return jax.shard_map(
        fused,
        mesh=mesh,
        in_specs=(rows, rows, rows, banks, banks, banks),
        out_specs=rows,
        check_vma=False,
    )
```

```python
import functools

import jax
import jax.numpy as jnp
from jax import lax
from jax.experimental import pallas as pl
from jax.experimental.pallas import tpu as pltpu
from jax.sharding import PartitionSpec as P

MESH = pl.DeviceIdType.MESH


def routing(expert_ids, combine, experts):
    rows = expert_ids.shape[0]
    named = expert_ids.T[:, None, :] == jnp.arange(experts, dtype=jnp.int32)[None, :, None]
    member = jnp.sum(named.astype(jnp.float32), axis=0)
    weight = jnp.sum(jnp.where(named, combine.T[:, None, :], 0.0), axis=0)
    before = (jnp.arange(rows)[:, None] < jnp.arange(rows)[None, :]).astype(jnp.bfloat16)
    rank = jnp.dot(member.astype(jnp.bfloat16), before, preferred_element_type=jnp.float32)
    return jnp.where(member > 0, rank, -1.0), weight


def plain(tokens, expert_ids, combine, gate_w, up_w, down_w):
    rows, features = tokens.shape
    groups = lax.axis_size("group")
    members = lax.axis_size("local")
    experts = groups * members
    capacity = max(2, rows * expert_ids.shape[1] * 5 // (4 * experts))
    slot, weight = routing(expert_ids, combine, experts)
    table = jnp.stack([slot, weight]).reshape(2, groups, members, rows)
    table = lax.all_to_all(table, "group", split_axis=1, concat_axis=1, tiled=True)
    slot, weight = table[0], table[1]
    blocks = lax.all_gather(tokens, "group")
    picks = slot[:, :, None, :] == jnp.arange(capacity, dtype=jnp.float32)[None, None, :, None]
    chosen = jnp.einsum(
        "blct,btd->blcd", picks.astype(jnp.bfloat16), blocks, preferred_element_type=jnp.float32
    ).astype(jnp.bfloat16)
    arrived = lax.all_to_all(chosen, "local", split_axis=1, concat_axis=1, tiled=True)
    x = arrived.reshape(-1, features)
    gate_part = jnp.dot(x, gate_w[0], preferred_element_type=jnp.float32)
    up_part = jnp.dot(x, up_w[0], preferred_element_type=jnp.float32)
    hidden = (jax.nn.silu(gate_part) * up_part).astype(jnp.bfloat16)
    result = jnp.dot(hidden, down_w[0], preferred_element_type=jnp.float32).astype(jnp.bfloat16)
    returned = lax.all_to_all(
        result.reshape(arrived.shape), "local", split_axis=1, concat_axis=1, tiled=True
    ).reshape(groups, members * capacity, features)
    mix = jnp.where(picks, weight[:, :, None, :], 0.0).reshape(groups, members * capacity, rows)
    high = mix.astype(jnp.bfloat16)
    low = (mix - high.astype(jnp.float32)).astype(jnp.bfloat16)
    part = jnp.einsum("bct,bcd->btd", high, returned, preferred_element_type=jnp.float32)
    part = part + jnp.einsum("bct,bcd->btd", low, returned, preferred_element_type=jnp.float32)
    return lax.psum_scatter(part.astype(jnp.bfloat16), "group", scatter_dimension=0, tiled=False)


def layer(capacity, lead, ids, combine, tokens, gate_w, up_w, down_w, out,
          block, tables, near_tables, picks, sending, rows, back, gate, up, down, hidden, mix,
          parts, lead_parts, chain, lead_chain, total,
          load_sem, t_send, t_recv, n_send, n_recv, z_send, z_recv, a_send, a_recv,
          x_send, x_recv, r_send, r_recv, e_send, e_recv, p_send, p_recv):
    groups, members = 4, 8
    g = lax.axis_index("group")
    me = lax.axis_index("local")
    at_y, at_x, at_c = me // 4, lax.rem(me // 2, 2), lax.rem(me, 2)
    count, features = tokens.shape
    experts = groups * members
    piece_rows = 2 * capacity
    width = 4 * piece_rows
    half = features // 2
    wide = 512
    half_tiles = (half - lead) // wide
    tiles = 2 * half_tiles
    f32, bf16 = jnp.float32, jnp.bfloat16

    def group_at(j):
        return lax.rem(g + j, groups)

    def at(y, x, c):
        return 4 * lax.rem(at_y + y, 2) + 2 * lax.rem(at_x + x, 2) + lax.rem(at_c + c, 2)

    def first(h):
        return at(h, 1 - h, 0)

    def partner(h, p):
        second = p // 2
        return at(second * (1 - h), second * h, lax.rem(p, 2))

    starts = (0, lead, half, features - lead)
    sizes = (lead, half - lead, half - lead, lead)

    def span(u):
        return pl.ds(starts[u], sizes[u])

    def tile(n):
        return pl.ds(pl.multiple_of(lead + n * wide, 128), wide)

    def packed(n):
        return pl.ds(pl.multiple_of(n * wide, 128), wide)

    def piece(p):
        return pl.ds(pl.multiple_of(p * piece_rows, 16), piece_rows)

    own, near, pair = pl.ds(0, count), pl.ds(count, count), pl.ds(0, 2 * count)

    def remote(src, dst, send, recv, group, local):
        return pltpu.make_async_remote_copy(
            src_ref=src, dst_ref=dst, send_sem=send, recv_sem=recv,
            device_id=(group, local), device_id_type=MESH)

    before_me = group_at(groups - 1)

    def t_copy(j):
        return remote(tables.at[j - 1], tables.at[j], t_send.at[j], t_recv.at[j], before_me, me)

    def n_copy(j, h):
        return remote(tables.at[j, g], near_tables.at[j, h], n_send.at[j, h], n_recv.at[j, h],
                      g, first(h))

    def z_copy(j, u):
        which = own if u in (1, 2) else pair
        return remote(block.at[j - 1, which, span(u)], block.at[j, which, span(u)],
                      z_send.at[j, u], z_recv.at[j, u], before_me, me)

    def a_copy(j, u):
        return remote(block.at[j, own, span(u)], block.at[j, near, span(u)],
                      a_send.at[j, u], a_recv.at[j, u], g, first(u // 2))

    def x_copy(j, u, p):
        return remote(sending.at[lax.min(j, 1), piece(p - 1), span(u)], rows.at[j, piece(p), span(u)],
                      x_send.at[j, u, p], x_recv.at[j, u, p], g, partner(u // 2, p))

    def wide_tile(k):
        n = lax.rem(k, 2) * half_tiles + k // 2
        return tile(n), lax.rem(k, 2), n

    def lead_tile(h):
        return span(3 * h), h, tiles + h

    def r_copy(j, of, p):
        cols, h, n = of
        return remote(rows.at[j, piece(p), cols], back.at[j, piece(p), cols],
                      r_send.at[j, n, p], r_recv.at[j, n, p], g, partner(h, p))

    def e_copy(j, of):
        cols, h, n = of
        landing = lead_parts.at[h] if isinstance(h, int) else parts.at[j, :, packed(n)]
        return remote(block.at[j, near, cols], landing,
                      e_send.at[j, n], e_recv.at[j, n], g, first(h))

    def p_copy(j, n):
        return remote(block.at[j, own, tile(n)], chain.at[j - 1, :, packed(n)],
                      p_send.at[j, n], p_recv.at[j, n], before_me, me)

    def q_copy(j, h):
        return remote(block.at[j, pair, span(3 * h)], lead_chain.at[j - 1, h],
                      p_send.at[j, tiles + h], p_recv.at[j, tiles + h], before_me, me)

    loads = [
        pltpu.make_async_copy(tokens, block.at[0, own], load_sem.at[0]),
        pltpu.make_async_copy(gate_w, gate, load_sem.at[1]),
        pltpu.make_async_copy(up_w, up, load_sem.at[2]),
        pltpu.make_async_copy(down_w, down, load_sem.at[3]),
    ]
    loads[0].start()
    barrier = pltpu.get_barrier_semaphore()
    peers = [(g, partner(h, p)) for h in range(2) for p in (1, 2, 3) if (h, p) != (1, 1)]
    peers += [(group_at(1), me), (before_me, me)]
    for peer in peers:
        pl.semaphore_signal(barrier, inc=1, device_id=peer, device_id_type=MESH)

    def iota(shape, axis):
        return lax.broadcasted_iota(jnp.int32, shape, axis)

    member = jnp.zeros((experts, count), f32)
    weight = jnp.zeros((experts, count), f32)
    for k in range(ids.shape[0]):
        named = ids[k : k + 1, :] == iota((experts, count), 0)
        member = member + jnp.where(named, 1.0, 0.0)
        weight = weight + jnp.where(named, combine[k : k + 1, :], 0.0)
    before = jnp.where(iota((count, count), 0) < iota((count, count), 1), 1.0, 0.0).astype(bf16)
    rank = jnp.dot(member.astype(bf16), before, preferred_element_type=f32)
    slot = jnp.where(member > 0, rank, -1.0 - capacity)
    for q in range(groups):
        tables[0, q, 0:members] = slot[q * members : (q + 1) * members]
        tables[0, q, members : 2 * members] = weight[q * members : (q + 1) * members]

    pl.semaphore_wait(barrier, len(peers))
    loads[0].wait()

    def slots_of(j, h):
        lanes = []
        for p in range(4):
            e = partner(h, p)
            near_slot = near_tables[j, h, pl.ds(e, 1), :] + float(capacity)
            lanes.append(jnp.concatenate([tables[j, g, pl.ds(e, 1), :], near_slot], axis=1))
        return lanes

    def weights_of(j, h):
        lanes = []
        for p in range(4):
            e = members + partner(h, p)
            lanes.append(jnp.concatenate(
                [tables[j, g, pl.ds(e, 1), :], near_tables[j, h, pl.ds(e, 1), :]], axis=1))
        return lanes

    def places():
        return iota((piece_rows, 2 * count), 0).astype(f32)

    def begin(j):
        @pl.when(j >= 1)
        def _():
            t_copy(j).wait()

        for h in range(2):
            n_copy(j, h).start()

        @pl.when(j + 1 < groups)
        def _():
            t_copy(j + 1).start()

        @pl.when(j == 0)
        def _():
            for u in (0, 3):
                a_copy(j, u).start()

        for u in (1, 2):
            @pl.when(j >= 1)
            def _():
                z_copy(j, u).wait()

            a_copy(j, u).start()

            @pl.when(j + 1 < groups)
            def _():
                z_copy(j + 1, u).start()

    def pick(j, u):
        h = u // 2

        def choose(cols):
            chosen = jnp.dot(
                picks[h], block[j, :, cols], preferred_element_type=f32).astype(bf16)
            rows[j, 0:piece_rows, cols] = chosen[0:piece_rows]
            sending[lax.min(j, 1), :, cols] = chosen[piece_rows:width]

        if u in (1, 2):
            @pl.loop(h * half_tiles, (h + 1) * half_tiles)
            def _(n):
                choose(tile(n))
        else:
            choose(span(u))
        for p in (2, 3, 1):
            x_copy(j, u, p).start()

    def prepare(j):
        for h in range(2):
            n_copy(j, h).wait()
            picks[h] = jnp.concatenate(
                [jnp.where(slot == places(), 1.0, 0.0) for slot in slots_of(j, h)], axis=0
            ).astype(bf16)

    def dispatch(j):
        for u in (1, 2):
            a_copy(j, u).wait()
            pick(j, u)

    def leads(j):
        for u in (0, 3):
            @pl.when(j == 0)
            def _():
                a_copy(j, u).wait()

            @pl.when(j >= 1)
            def _():
                z_copy(j, u).wait()

            @pl.when(j + 1 < groups)
            def _():
                z_copy(j + 1, u).start()
        for u in (0, 3):
            pick(j, u)

    def swapped(v):
        groups_of = [v[k * capacity : (k + 1) * capacity] for k in range(8)]
        return jnp.concatenate(
            [groups_of[4 * k + 2 * c + s] for s in range(2) for c in range(2) for k in range(2)], axis=0)

    def compute(j):
        @pl.when(j == 1)
        def _():
            loads[1].wait()
            loads[2].wait()
            loads[3].wait()

        for u in range(4):
            for p in (1, 2, 3):
                x_copy(j, u, p).wait()

        units = hidden.shape[2]

        @pl.loop(0, units // 256)
        def _(n):
            cols = pl.ds(pl.multiple_of(n * 256, 256), 256)

            def project(bank):
                left = jnp.dot(rows[j, :, 0:half], bank[0:half, cols], preferred_element_type=f32)
                right = jnp.dot(rows[j, :, half:features], bank[half:features, cols],
                                preferred_element_type=f32)
                return left + swapped(right)

            a = project(gate)
            b = project(up)
            value = jax.nn.silu(a) * b
            hidden[0, :, cols] = value.astype(bf16)
            hidden[1, :, cols] = swapped(value).astype(bf16)

        def project_back(of):
            cols, h, _ = of
            result = jnp.dot(hidden[h], down[:, cols], preferred_element_type=f32).astype(bf16)
            back[j, 0:piece_rows, cols] = result[0:piece_rows]
            rows[j, piece_rows:width, cols] = result[piece_rows:width]
            @pl.when(j >= 1)
            def _():
                send_back(j, of)

        for h in range(2):
            project_back(lead_tile(h))

        @pl.loop(0, tiles)
        def _(n):
            project_back(wide_tile(n))

    def send_back(j, of):
        for p in (2, 3, 1):
            r_copy(j, of, p).start()

    def send_all(j):
        for h in range(2):
            send_back(j, lead_tile(h))

        @pl.loop(0, tiles)
        def _(n):
            send_back(j, wide_tile(n))

    def gather(j, last):
        unit = jnp.where(iota((2 * count, 2 * count), 0) == iota((2 * count, 2 * count), 1), 1.0, 0.0).astype(bf16)
        for h in range(2):
            weights = jnp.concatenate(
                [jnp.where(slot == places(), weight, 0.0)
                 for slot, weight in zip(slots_of(j, h), weights_of(j, h))], axis=0)
            mix[h] = lax.dot_general(
                unit, weights.astype(bf16), (((1,), (1,)), ((), ())),
                preferred_element_type=f32).astype(bf16)

        def mixed(of):
            cols, h, _ = of
            for p in (1, 2, 3):
                r_copy(j, of, p).wait()
            return jnp.dot(mix[h], back[j, :, cols], preferred_element_type=f32)

        for h in range(2):
            of = lead_tile(h)
            both = mixed(of)
            if last:
                q_copy(groups - 1, h).wait()
                both = both + lead_chain[groups - 2, h].astype(f32)
                block[j, near, of[0]] = both[count : 2 * count].astype(bf16)
                e_copy(j, of).start()
                total[:, of[0]] = both[0:count]
            else:
                @pl.when(j == 1)
                def _():
                    block[j, :, of[0]] = both.astype(bf16)

                @pl.when(j >= 2)
                def _():
                    q_copy(j - 1, h).wait()
                    block[j, :, of[0]] = (both + lead_chain[j - 2, h].astype(f32)).astype(bf16)

                q_copy(j, h).start()

        @pl.loop(0, tiles)
        def _(n):
            of = wide_tile(n)
            both = mixed(of)
            block[j, near, of[0]] = both[count : 2 * count].astype(bf16)
            e_copy(j, of).start()
            total[:, of[0]] = both[0:count]

    def arrived(j, n):
        return chain[j, :, packed(n)].astype(f32)

    def finish(j):
        @pl.loop(0, tiles)
        def _(k):
            n = wide_tile(k)[2]
            e_copy(j, wide_tile(k)).wait()
            part = total[:, tile(n)] + parts[j, :, packed(n)].astype(f32)

            @pl.when(j == 1)
            def _():
                block[j, own, tile(n)] = part.astype(bf16)

            @pl.when(j >= 2)
            def _():
                p_copy(j - 1, n).wait()
                block[j, own, tile(n)] = (part + arrived(j - 2, n)).astype(bf16)

            p_copy(j, n).start()

    for load in loads[1:]:
        load.start()
    plan = (
        ("begin", 0), ("prepare", 0), ("leads", 0), ("dispatch", 0), ("begin", 1), ("prepare", 1),
        ("dispatch", 1), ("leads", 1), ("begin", 2), ("compute", 1), ("prepare", 2), ("dispatch", 2),
        ("leads", 2), ("compute", 0), ("begin", 3), ("gather", 1), ("compute", 2), ("prepare", 3),
        ("dispatch", 3), ("finish", 1), ("leads", 3), ("gather", 2), ("compute", 3), ("finish", 2),
        ("gather", 3), ("send", 0), ("finish", 3),
    )
    acts = {"begin": begin, "prepare": prepare, "dispatch": dispatch, "leads": leads, "compute": compute,
            "gather": lambda j: gather(j, False), "finish": finish, "send": send_all}

    @pl.loop(0, len(plan))
    def _(step):
        for name, act in acts.items():
            at_steps = [(k, j) for k, (other, j) in enumerate(plan) if other == name]
            if not at_steps:
                continue
            now, which = False, 0
            for k, j in at_steps:
                now = (step == k) | now
                which = which + jnp.where(step == k, j, 0)

            @pl.when(now)
            def _(act=act, which=which):
                act(which)

    gather(0, True)
    for h in range(2):
        cols = lead_tile(h)[0]
        e_copy(0, lead_tile(h)).wait()
        out[:, cols] = (total[:, cols] + lead_parts[h].astype(f32)).astype(bf16)

    @pl.loop(0, tiles)
    def _(k):
        n = wide_tile(k)[2]
        e_copy(0, wide_tile(k)).wait()
        p_copy(groups - 1, n).wait()
        out[:, tile(n)] = (
            total[:, tile(n)] + parts[0, :, packed(n)].astype(f32) + arrived(groups - 2, n)).astype(bf16)


def fused(tokens, expert_ids, combine, gate_w, up_w, down_w):
    count, features = tokens.shape
    units = gate_w.shape[2]
    groups = lax.axis_size("group")
    members = lax.axis_size("local")
    experts = groups * members
    capacity = max(2, count * expert_ids.shape[1] * 5 // (4 * experts))
    if (groups, members) != (4, 8) or capacity % 8 or features % 2048 or units % 256 or count % 128:
        return plain(tokens, expert_ids, combine, gate_w, up_w, down_w)
    width = members * capacity
    lead = features // 8
    slots = 2 * ((features // 2 - lead) // 512) + 2
    half = jnp.bfloat16
    dma = pltpu.SemaphoreType.DMA
    anywhere = pl.BlockSpec(memory_space=pl.ANY)
    inside = pl.BlockSpec(memory_space=pltpu.VMEM)
    return pl.pallas_call(
        functools.partial(layer, capacity, lead),
        out_shape=jax.ShapeDtypeStruct((count, features), half),
        in_specs=[inside, inside, anywhere, anywhere, anywhere, anywhere],
        out_specs=inside,
        scratch_shapes=[
            pltpu.VMEM((groups, 2 * count, features), half),
            pltpu.VMEM((groups, groups, 2 * members, count), jnp.float32),
            pltpu.VMEM((groups, 2, 2 * members, count), jnp.float32),
            pltpu.VMEM((2, width, 2 * count), half),
            pltpu.VMEM((2, width * 3 // 4, features), half),
            pltpu.VMEM((groups, width, features), half),
            pltpu.VMEM((groups, width, features), half),
            pltpu.VMEM((features, units), half),
            pltpu.VMEM((features, units), half),
            pltpu.VMEM((units, features), half),
            pltpu.VMEM((2, width, units), half),
            pltpu.VMEM((2, 2 * count, width), half),
            pltpu.VMEM((groups, count, features - 2 * lead), half),
            pltpu.VMEM((2, count, lead), half),
            pltpu.VMEM((groups - 1, count, features - 2 * lead), half),
            pltpu.VMEM((groups - 1, 2, 2 * count, lead), half),
            pltpu.VMEM((count, features), jnp.float32),
            dma((4,)),
            dma((groups,)), dma((groups,)),
            dma((groups, 2)), dma((groups, 2)),
            dma((groups, 4)), dma((groups, 4)),
            dma((groups, 4)), dma((groups, 4)),
            dma((groups, 4, 4)), dma((groups, 4, 4)),
            dma((groups, slots, 4)), dma((groups, slots, 4)),
            dma((groups, slots)), dma((groups, slots)),
            dma((groups, slots)), dma((groups, slots)),
        ],
        compiler_params=pltpu.CompilerParams(
            collective_id=0, has_side_effects=True, vmem_limit_bytes=63 * 1024 * 1024),
    )(expert_ids.T, combine.T, tokens, gate_w[0], up_w[0], down_w[0])


def solution(mesh):
    rows = P(("group", "local"), None)
    banks = P(("group", "local"), None, None)
    return jax.shard_map(
        fused,
        mesh=mesh,
        in_specs=(rows, rows, rows, banks, banks, banks),
        out_specs=rows,
        check_vma=False,
    )
```

```python
import functools

import jax
import jax.numpy as jnp
from jax import lax
from jax.experimental import pallas as pl
from jax.experimental.pallas import tpu as pltpu
from jax.sharding import PartitionSpec as P

MESH = pl.DeviceIdType.MESH


def routing(expert_ids, combine, experts):
    rows = expert_ids.shape[0]
    named = expert_ids.T[:, None, :] == jnp.arange(experts, dtype=jnp.int32)[None, :, None]
    member = jnp.sum(named.astype(jnp.float32), axis=0)
    weight = jnp.sum(jnp.where(named, combine.T[:, None, :], 0.0), axis=0)
    before = (jnp.arange(rows)[:, None] < jnp.arange(rows)[None, :]).astype(jnp.bfloat16)
    rank = jnp.dot(member.astype(jnp.bfloat16), before, preferred_element_type=jnp.float32)
    return jnp.where(member > 0, rank, -1.0), weight


def plain(tokens, expert_ids, combine, gate_w, up_w, down_w):
    rows, features = tokens.shape
    groups = lax.axis_size("group")
    members = lax.axis_size("local")
    experts = groups * members
    capacity = max(2, rows * expert_ids.shape[1] * 5 // (4 * experts))
    slot, weight = routing(expert_ids, combine, experts)
    table = jnp.stack([slot, weight]).reshape(2, groups, members, rows)
    table = lax.all_to_all(table, "group", split_axis=1, concat_axis=1, tiled=True)
    slot, weight = table[0], table[1]
    blocks = lax.all_gather(tokens, "group")
    picks = slot[:, :, None, :] == jnp.arange(capacity, dtype=jnp.float32)[None, None, :, None]
    chosen = jnp.einsum(
        "blct,btd->blcd", picks.astype(jnp.bfloat16), blocks, preferred_element_type=jnp.float32
    ).astype(jnp.bfloat16)
    arrived = lax.all_to_all(chosen, "local", split_axis=1, concat_axis=1, tiled=True)
    x = arrived.reshape(-1, features)
    gate_part = jnp.dot(x, gate_w[0], preferred_element_type=jnp.float32)
    up_part = jnp.dot(x, up_w[0], preferred_element_type=jnp.float32)
    hidden = (jax.nn.silu(gate_part) * up_part).astype(jnp.bfloat16)
    result = jnp.dot(hidden, down_w[0], preferred_element_type=jnp.float32).astype(jnp.bfloat16)
    returned = lax.all_to_all(
        result.reshape(arrived.shape), "local", split_axis=1, concat_axis=1, tiled=True
    ).reshape(groups, members * capacity, features)
    mix = jnp.where(picks, weight[:, :, None, :], 0.0).reshape(groups, members * capacity, rows)
    high = mix.astype(jnp.bfloat16)
    low = (mix - high.astype(jnp.float32)).astype(jnp.bfloat16)
    part = jnp.einsum("bct,bcd->btd", high, returned, preferred_element_type=jnp.float32)
    part = part + jnp.einsum("bct,bcd->btd", low, returned, preferred_element_type=jnp.float32)
    return lax.psum_scatter(part.astype(jnp.bfloat16), "group", scatter_dimension=0, tiled=False)


def layer(capacity, ahead, lead, ids, combine, tokens, gate_w, up_w, down_w, out,
          block, tables, near_tables, picks, sending, rows, back, gate, up, down, hidden, mix,
          parts, lead_parts, chain, lead_chain, total,
          load_sem, out_sem, t_send, t_recv, n_send, n_recv, z_send, z_recv, a_send, a_recv,
          x_send, x_recv, r_send, r_recv, e_send, e_recv, p_send, p_recv):
    groups, members = 4, 8
    g = lax.axis_index("group")
    me = lax.axis_index("local")
    at_y, at_x, at_c = me // 4, lax.rem(me // 2, 2), lax.rem(me, 2)
    count, features = tokens.shape
    experts = groups * members
    piece_rows = 2 * capacity
    width = 4 * piece_rows
    half = features // 2
    wide = 640
    half_tiles = (half - lead) // wide
    pick_wide = 1408
    half_picks = (half - ahead) // pick_wide
    tiles = 2 * half_tiles
    f32, bf16 = jnp.float32, jnp.bfloat16

    def group_at(j):
        return lax.rem(g + j, groups)

    def at(y, x, c):
        return 4 * lax.rem(at_y + y, 2) + 2 * lax.rem(at_x + x, 2) + lax.rem(at_c + c, 2)

    def first(h):
        return at(h, 1 - h, 0)

    def partner(h, p):
        second = p // 2
        return at(second * (1 - h), second * h, lax.rem(p, 2))

    starts = (0, ahead, half, features - ahead)
    sizes = (ahead, half - ahead, half - ahead, ahead)

    def span(u):
        return pl.ds(starts[u], sizes[u])

    def tile(n):
        return pl.ds(pl.multiple_of(lead + n * wide, 128), wide)

    def packed(n):
        return pl.ds(pl.multiple_of(n * wide, 128), wide)

    def piece(p):
        return pl.ds(pl.multiple_of(p * piece_rows, 16), piece_rows)

    own, near, pair = pl.ds(0, count), pl.ds(count, count), pl.ds(0, 2 * count)

    def remote(src, dst, send, recv, group, local):
        return pltpu.make_async_remote_copy(
            src_ref=src, dst_ref=dst, send_sem=send, recv_sem=recv,
            device_id=(group, local), device_id_type=MESH)

    before_me = group_at(groups - 1)

    def t_copy(j):
        return remote(tables.at[j - 1], tables.at[j], t_send.at[j], t_recv.at[j], before_me, me)

    def n_copy(j, h):
        return remote(tables.at[j, g], near_tables.at[j, h], n_send.at[j, h], n_recv.at[j, h],
                      g, first(h))

    def z_copy(j, u):
        which = own if u in (1, 2) else pair
        return remote(block.at[j - 1, which, span(u)], block.at[j, which, span(u)],
                      z_send.at[j, u], z_recv.at[j, u], before_me, me)

    def a_copy(j, u):
        return remote(block.at[j, own, span(u)], block.at[j, near, span(u)],
                      a_send.at[j, u], a_recv.at[j, u], g, first(u // 2))

    def x_copy(j, u, p):
        return remote(sending.at[lax.min(j, 1), piece(p - 1), span(u)], rows.at[j, piece(p), span(u)],
                      x_send.at[j, u, p], x_recv.at[j, u, p], g, partner(u // 2, p))

    def wide_tile(k):
        n = lax.rem(k, 2) * half_tiles + k // 2
        return tile(n), lax.rem(k, 2), n

    def lead_tile(h):
        return pl.ds(h * (features - lead), lead), h, tiles + h

    def r_copy(j, of, p):
        cols, h, n = of
        return remote(rows.at[j, piece(p), cols], back.at[j, piece(p), cols],
                      r_send.at[j, n, p], r_recv.at[j, n, p], g, partner(h, p))

    def e_copy(j, of):
        cols, h, n = of
        landing = lead_parts.at[h] if isinstance(h, int) else parts.at[j, :, packed(n)]
        return remote(block.at[j, near, cols], landing,
                      e_send.at[j, n], e_recv.at[j, n], g, first(h))

    def p_copy(j, n):
        return remote(block.at[j, own, tile(n)], chain.at[j - 1, :, packed(n)],
                      p_send.at[j, n], p_recv.at[j, n], before_me, me)

    def q_copy(j, h):
        return remote(block.at[j, pair, lead_tile(h)[0]], lead_chain.at[j - 1, h],
                      p_send.at[j, tiles + h], p_recv.at[j, tiles + h], before_me, me)

    loads = [
        pltpu.make_async_copy(tokens, block.at[0, own], load_sem.at[0]),
        pltpu.make_async_copy(gate_w, gate, load_sem.at[1]),
        pltpu.make_async_copy(up_w, up, load_sem.at[2]),
        pltpu.make_async_copy(down_w, down, load_sem.at[3]),
    ]
    loads[0].start()
    barrier = pltpu.get_barrier_semaphore()
    peers = [(g, partner(h, p)) for h in range(2) for p in (1, 2, 3) if (h, p) != (1, 1)]
    peers += [(group_at(1), me), (before_me, me)]
    for peer in peers:
        pl.semaphore_signal(barrier, inc=1, device_id=peer, device_id_type=MESH)

    def iota(shape, axis):
        return lax.broadcasted_iota(jnp.int32, shape, axis)

    member = jnp.zeros((experts, count), f32)
    weight = jnp.zeros((experts, count), f32)
    for k in range(ids.shape[0]):
        named = ids[k : k + 1, :] == iota((experts, count), 0)
        member = member + jnp.where(named, 1.0, 0.0)
        weight = weight + jnp.where(named, combine[k : k + 1, :], 0.0)
    before = jnp.where(iota((count, count), 0) < iota((count, count), 1), 1.0, 0.0).astype(bf16)
    rank = jnp.dot(member.astype(bf16), before, preferred_element_type=f32)
    slot = jnp.where(member > 0, rank, -1.0 - capacity)
    for q in range(groups):
        tables[0, q, 0:members] = slot[q * members : (q + 1) * members]
        tables[0, q, members : 2 * members] = weight[q * members : (q + 1) * members]

    pl.semaphore_wait(barrier, len(peers))
    loads[0].wait()

    def slots_of(j, h):
        lanes = []
        for p in range(4):
            e = partner(h, p)
            near_slot = near_tables[j, h, pl.ds(e, 1), :] + float(capacity)
            lanes.append(jnp.concatenate([tables[j, g, pl.ds(e, 1), :], near_slot], axis=1))
        return lanes

    def weights_of(j, h):
        lanes = []
        for p in range(4):
            e = members + partner(h, p)
            lanes.append(jnp.concatenate(
                [tables[j, g, pl.ds(e, 1), :], near_tables[j, h, pl.ds(e, 1), :]], axis=1))
        return lanes

    def places():
        return iota((piece_rows, 2 * count), 0).astype(f32)

    def begin(j):
        @pl.when(j >= 1)
        def _():
            t_copy(j).wait()

        for h in range(2):
            n_copy(j, h).start()

        @pl.when(j + 1 < groups)
        def _():
            t_copy(j + 1).start()

        @pl.when(j == 0)
        def _():
            for u in (0, 3):
                a_copy(j, u).start()

        for u in (1, 2):
            @pl.when(j >= 1)
            def _():
                z_copy(j, u).wait()

            a_copy(j, u).start()

            @pl.when(j + 1 < groups)
            def _():
                z_copy(j + 1, u).start()

    def pick(j, u):
        h = u // 2

        def choose(cols):
            chosen = jnp.dot(
                picks[h], block[j, :, cols], preferred_element_type=f32).astype(bf16)
            rows[j, 0:piece_rows, cols] = chosen[0:piece_rows]
            sending[lax.min(j, 1), :, cols] = chosen[piece_rows:width]

        if u in (1, 2):
            @pl.loop(h * half_picks, (h + 1) * half_picks)
            def _(n):
                choose(pl.ds(pl.multiple_of(ahead + n * pick_wide, 128), pick_wide))
        else:
            choose(span(u))
        for p in (2, 3, 1):
            x_copy(j, u, p).start()

    def prepare(j):
        for h in range(2):
            n_copy(j, h).wait()
            picks[h] = jnp.concatenate(
                [jnp.where(slot == places(), 1.0, 0.0) for slot in slots_of(j, h)], axis=0
            ).astype(bf16)

    def dispatch(j):
        for u in (1, 2):
            a_copy(j, u).wait()
            pick(j, u)

    def leads(j):
        for u in (0, 3):
            @pl.when(j == 0)
            def _():
                a_copy(j, u).wait()

            @pl.when(j >= 1)
            def _():
                z_copy(j, u).wait()

            @pl.when(j + 1 < groups)
            def _():
                z_copy(j + 1, u).start()
        for u in (0, 3):
            pick(j, u)

    def swapped(v):
        groups_of = [v[k * capacity : (k + 1) * capacity] for k in range(8)]
        return jnp.concatenate(
            [groups_of[4 * k + 2 * c + s] for s in range(2) for c in range(2) for k in range(2)], axis=0)

    def compute(j):
        @pl.when(j == 1)
        def _():
            loads[1].wait()
            loads[2].wait()
            loads[3].wait()

        for u in range(4):
            for p in (1, 2, 3):
                x_copy(j, u, p).wait()

        units = hidden.shape[2]

        @pl.loop(0, units // 256)
        def _(n):
            cols = pl.ds(pl.multiple_of(n * 256, 256), 256)

            def project(bank):
                left = jnp.dot(rows[j, :, 0:half], bank[0:half, cols], preferred_element_type=f32)
                right = jnp.dot(rows[j, :, half:features], bank[half:features, cols],
                                preferred_element_type=f32)
                return left + swapped(right)

            a = project(gate)
            b = project(up)
            value = jax.nn.silu(a) * b
            hidden[0, :, cols] = value.astype(bf16)
            hidden[1, :, cols] = swapped(value).astype(bf16)

        def project_back(of):
            cols, h, _ = of
            result = jnp.dot(hidden[h], down[:, cols], preferred_element_type=f32).astype(bf16)
            back[j, 0:piece_rows, cols] = result[0:piece_rows]
            rows[j, piece_rows:width, cols] = result[piece_rows:width]
            @pl.when(j >= 1)
            def _():
                send_back(j, of)

        for h in range(2):
            project_back(lead_tile(h))

        @pl.loop(0, tiles)
        def _(n):
            project_back(wide_tile(n))

    def send_back(j, of):
        for p in (2, 3, 1):
            r_copy(j, of, p).start()

    def send_all(j):
        for h in range(2):
            send_back(j, lead_tile(h))

        @pl.loop(0, tiles)
        def _(n):
            send_back(j, wide_tile(n))

    def gather(j, last):
        unit = jnp.where(iota((2 * count, 2 * count), 0) == iota((2 * count, 2 * count), 1), 1.0, 0.0).astype(bf16)
        for h in range(2):
            weights = jnp.concatenate(
                [jnp.where(slot == places(), weight, 0.0)
                 for slot, weight in zip(slots_of(j, h), weights_of(j, h))], axis=0)
            mix[h] = lax.dot_general(
                unit, weights.astype(bf16), (((1,), (1,)), ((), ())),
                preferred_element_type=f32).astype(bf16)

        def mixed(of):
            cols, h, _ = of
            for p in (1, 2, 3):
                r_copy(j, of, p).wait()
            return jnp.dot(mix[h], back[j, :, cols], preferred_element_type=f32)

        for h in range(2):
            of = lead_tile(h)
            both = mixed(of)
            if last:
                q_copy(groups - 1, h).wait()
                both = both + lead_chain[groups - 2, h].astype(f32)
                block[j, near, of[0]] = both[count : 2 * count].astype(bf16)
                e_copy(j, of).start()
                total[:, of[0]] = both[0:count]
            else:
                @pl.when(j == 1)
                def _():
                    block[j, :, of[0]] = both.astype(bf16)

                @pl.when(j >= 2)
                def _():
                    q_copy(j - 1, h).wait()
                    block[j, :, of[0]] = (both + lead_chain[j - 2, h].astype(f32)).astype(bf16)

                q_copy(j, h).start()

        @pl.loop(0, tiles)
        def _(n):
            of = wide_tile(n)
            both = mixed(of)
            block[j, near, of[0]] = both[count : 2 * count].astype(bf16)
            e_copy(j, of).start()
            total[:, of[0]] = both[0:count]

    def arrived(j, n):
        return chain[j, :, packed(n)].astype(f32)

    def finish(j):
        @pl.loop(0, tiles)
        def _(k):
            n = wide_tile(k)[2]
            e_copy(j, wide_tile(k)).wait()
            part = total[:, tile(n)] + parts[j, :, packed(n)].astype(f32)

            @pl.when(j == 1)
            def _():
                block[j, own, tile(n)] = part.astype(bf16)

            @pl.when(j >= 2)
            def _():
                p_copy(j - 1, n).wait()
                block[j, own, tile(n)] = (part + arrived(j - 2, n)).astype(bf16)

            p_copy(j, n).start()

    for load in loads[1:]:
        load.start()
    plan = (
        ("begin", 0), ("prepare", 0), ("leads", 0), ("dispatch", 0), ("begin", 1), ("prepare", 1),
        ("dispatch", 1), ("leads", 1), ("begin", 2), ("compute", 1), ("prepare", 2), ("dispatch", 2),
        ("leads", 2), ("compute", 0), ("begin", 3), ("gather", 1), ("compute", 2), ("prepare", 3),
        ("dispatch", 3), ("finish", 1), ("leads", 3), ("gather", 2), ("compute", 3), ("finish", 2),
        ("gather", 3), ("send", 0), ("finish", 3),
    )
    acts = {"begin": begin, "prepare": prepare, "dispatch": dispatch, "leads": leads, "compute": compute,
            "gather": lambda j: gather(j, False), "finish": finish, "send": send_all}

    @pl.loop(0, len(plan))
    def _(step):
        for name, act in acts.items():
            at_steps = [(k, j) for k, (other, j) in enumerate(plan) if other == name]
            if not at_steps:
                continue
            now, which = False, 0
            for k, j in at_steps:
                now = (step == k) | now
                which = which + jnp.where(step == k, j, 0)

            @pl.when(now)
            def _(act=act, which=which):
                act(which)

    gather(0, True)

    def out_copy(of):
        return pltpu.make_async_copy(block.at[0, own, of[0]], out.at[:, of[0]], out_sem.at[of[2]])

    for h in range(2):
        of = lead_tile(h)
        e_copy(0, of).wait()
        block[0, own, of[0]] = (total[:, of[0]] + lead_parts[h].astype(f32)).astype(bf16)
        out_copy(of).start()

    @pl.loop(0, tiles)
    def _(k):
        of = wide_tile(k)
        e_copy(0, of).wait()
        p_copy(groups - 1, of[2]).wait()
        block[0, own, of[0]] = (
            total[:, of[0]] + parts[0, :, packed(of[2])].astype(f32) + arrived(groups - 2, of[2])).astype(bf16)
        out_copy(of).start()

    for h in range(2):
        out_copy(lead_tile(h)).wait()

    @pl.loop(0, tiles)
    def _(k):
        out_copy(wide_tile(k)).wait()


def fused(tokens, expert_ids, combine, gate_w, up_w, down_w):
    count, features = tokens.shape
    units = gate_w.shape[2]
    groups = lax.axis_size("group")
    members = lax.axis_size("local")
    experts = groups * members
    capacity = max(2, count * expert_ids.shape[1] * 5 // (4 * experts))
    if (groups, members) != (4, 8) or capacity % 8 or features % 2048 or units % 256 or count % 128:
        return plain(tokens, expert_ids, combine, gate_w, up_w, down_w)
    width = members * capacity
    lead = 768
    slots = 2 * ((features // 2 - lead) // 640) + 2
    half = jnp.bfloat16
    dma = pltpu.SemaphoreType.DMA
    anywhere = pl.BlockSpec(memory_space=pl.ANY)
    inside = pl.BlockSpec(memory_space=pltpu.VMEM)
    return pl.pallas_call(
        functools.partial(layer, capacity, 640, lead),
        out_shape=jax.ShapeDtypeStruct((count, features), half),
        in_specs=[inside, inside, anywhere, anywhere, anywhere, anywhere],
        out_specs=anywhere,
        scratch_shapes=[
            pltpu.VMEM((groups, 2 * count, features), half),
            pltpu.VMEM((groups, groups, 2 * members, count), jnp.float32),
            pltpu.VMEM((groups, 2, 2 * members, count), jnp.float32),
            pltpu.VMEM((2, width, 2 * count), half),
            pltpu.VMEM((2, width * 3 // 4, features), half),
            pltpu.VMEM((groups, width, features), half),
            pltpu.VMEM((groups, width, features), half),
            pltpu.VMEM((features, units), half),
            pltpu.VMEM((features, units), half),
            pltpu.VMEM((units, features), half),
            pltpu.VMEM((2, width, units), half),
            pltpu.VMEM((2, 2 * count, width), half),
            pltpu.VMEM((groups, count, features - 2 * lead), half),
            pltpu.VMEM((2, count, lead), half),
            pltpu.VMEM((groups - 1, count, features - 2 * lead), half),
            pltpu.VMEM((groups - 1, 2, 2 * count, lead), half),
            pltpu.VMEM((count, features), jnp.float32),
            dma((4,)), dma((slots,)),
            dma((groups,)), dma((groups,)),
            dma((groups, 2)), dma((groups, 2)),
            dma((groups, 4)), dma((groups, 4)),
            dma((groups, 4)), dma((groups, 4)),
            dma((groups, 4, 4)), dma((groups, 4, 4)),
            dma((groups, slots, 4)), dma((groups, slots, 4)),
            dma((groups, slots)), dma((groups, slots)),
            dma((groups, slots)), dma((groups, slots)),
        ],
        compiler_params=pltpu.CompilerParams(
            collective_id=0, has_side_effects=True, vmem_limit_bytes=63 * 1024 * 1024),
    )(expert_ids.T, combine.T, tokens, gate_w[0], up_w[0], down_w[0])


def solution(mesh):
    rows = P(("group", "local"), None)
    banks = P(("group", "local"), None, None)
    return jax.shard_map(
        fused,
        mesh=mesh,
        in_specs=(rows, rows, rows, banks, banks, banks),
        out_specs=rows,
        check_vma=False,
    )
```

```python
import functools

import jax
import jax.numpy as jnp
from jax import lax
from jax.experimental import pallas as pl
from jax.experimental.pallas import tpu as pltpu
from jax.sharding import PartitionSpec as P

MESH = pl.DeviceIdType.MESH


def routing(expert_ids, combine, experts):
    rows = expert_ids.shape[0]
    named = expert_ids.T[:, None, :] == jnp.arange(experts, dtype=jnp.int32)[None, :, None]
    member = jnp.sum(named.astype(jnp.float32), axis=0)
    weight = jnp.sum(jnp.where(named, combine.T[:, None, :], 0.0), axis=0)
    before = (jnp.arange(rows)[:, None] < jnp.arange(rows)[None, :]).astype(jnp.bfloat16)
    rank = jnp.dot(member.astype(jnp.bfloat16), before, preferred_element_type=jnp.float32)
    return jnp.where(member > 0, rank, -1.0), weight


def plain(tokens, expert_ids, combine, gate_w, up_w, down_w):
    rows, features = tokens.shape
    groups = lax.axis_size("group")
    members = lax.axis_size("local")
    experts = groups * members
    capacity = max(2, rows * expert_ids.shape[1] * 5 // (4 * experts))
    slot, weight = routing(expert_ids, combine, experts)
    table = jnp.stack([slot, weight]).reshape(2, groups, members, rows)
    table = lax.all_to_all(table, "group", split_axis=1, concat_axis=1, tiled=True)
    slot, weight = table[0], table[1]
    blocks = lax.all_gather(tokens, "group")
    picks = slot[:, :, None, :] == jnp.arange(capacity, dtype=jnp.float32)[None, None, :, None]
    chosen = jnp.einsum(
        "blct,btd->blcd", picks.astype(jnp.bfloat16), blocks, preferred_element_type=jnp.float32
    ).astype(jnp.bfloat16)
    arrived = lax.all_to_all(chosen, "local", split_axis=1, concat_axis=1, tiled=True)
    x = arrived.reshape(-1, features)
    gate_part = jnp.dot(x, gate_w[0], preferred_element_type=jnp.float32)
    up_part = jnp.dot(x, up_w[0], preferred_element_type=jnp.float32)
    hidden = (jax.nn.silu(gate_part) * up_part).astype(jnp.bfloat16)
    result = jnp.dot(hidden, down_w[0], preferred_element_type=jnp.float32).astype(jnp.bfloat16)
    returned = lax.all_to_all(
        result.reshape(arrived.shape), "local", split_axis=1, concat_axis=1, tiled=True
    ).reshape(groups, members * capacity, features)
    mix = jnp.where(picks, weight[:, :, None, :], 0.0).reshape(groups, members * capacity, rows)
    high = mix.astype(jnp.bfloat16)
    low = (mix - high.astype(jnp.float32)).astype(jnp.bfloat16)
    part = jnp.einsum("bct,bcd->btd", high, returned, preferred_element_type=jnp.float32)
    part = part + jnp.einsum("bct,bcd->btd", low, returned, preferred_element_type=jnp.float32)
    return lax.psum_scatter(part.astype(jnp.bfloat16), "group", scatter_dimension=0, tiled=False)


def layer(capacity, ahead, lead, ids, combine, tokens, gate_w, up_w, down_w, out,
          block, tables, near_tables, picks, sending, rows, back, gate, up, down, hidden, mix,
          parts, lead_parts, chain, lead_chain, total,
          load_sem, out_sem, t_send, t_recv, n_send, n_recv, z_send, z_recv, a_send, a_recv,
          x_send, x_recv, r_send, r_recv, e_send, e_recv, p_send, p_recv):
    groups, members = 4, 8
    g = lax.axis_index("group")
    me = lax.axis_index("local")
    at_y, at_x, at_c = me // 4, lax.rem(me // 2, 2), lax.rem(me, 2)
    count, features = tokens.shape
    experts = groups * members
    piece_rows = 2 * capacity
    width = 4 * piece_rows
    half = features // 2
    wide = 640
    half_tiles = (half - lead) // wide
    pick_wide = 1408
    half_picks = (half - ahead) // pick_wide
    tiles = 2 * half_tiles
    f32, bf16 = jnp.float32, jnp.bfloat16

    def group_at(j):
        return lax.rem(g + j, groups)

    def at(y, x, c):
        return 4 * lax.rem(at_y + y, 2) + 2 * lax.rem(at_x + x, 2) + lax.rem(at_c + c, 2)

    def first(h):
        return at(h, 1 - h, 0)

    def partner(h, p):
        second = p // 2
        return at(second * (1 - h), second * h, lax.rem(p, 2))

    starts = (0, ahead, half, features - ahead)
    sizes = (ahead, half - ahead, half - ahead, ahead)

    def span(u):
        return pl.ds(starts[u], sizes[u])

    def tile(n):
        return pl.ds(pl.multiple_of(lead + n * wide, 128), wide)

    def packed(n):
        return pl.ds(pl.multiple_of(n * wide, 128), wide)

    def piece(p):
        return pl.ds(pl.multiple_of(p * piece_rows, 16), piece_rows)

    own, near, pair = pl.ds(0, count), pl.ds(count, count), pl.ds(0, 2 * count)

    def remote(src, dst, send, recv, group, local):
        return pltpu.make_async_remote_copy(
            src_ref=src, dst_ref=dst, send_sem=send, recv_sem=recv,
            device_id=(group, local), device_id_type=MESH)

    before_me = group_at(groups - 1)

    def t_copy(j):
        return remote(tables.at[j - 1], tables.at[j], t_send.at[j], t_recv.at[j], before_me, me)

    def n_copy(j, h):
        return remote(tables.at[j, g], near_tables.at[j, h], n_send.at[j, h], n_recv.at[j, h],
                      g, first(h))

    def z_copy(j, u):
        which = own if u in (1, 2) else pair
        return remote(block.at[j - 1, which, span(u)], block.at[j, which, span(u)],
                      z_send.at[j, u], z_recv.at[j, u], before_me, me)

    def a_copy(j, u):
        return remote(block.at[j, own, span(u)], block.at[j, near, span(u)],
                      a_send.at[j, u], a_recv.at[j, u], g, first(u // 2))

    def x_copy(j, u, p):
        return remote(sending.at[lax.min(j, 1), piece(p - 1), span(u)], rows.at[j, piece(p), span(u)],
                      x_send.at[j, u, p], x_recv.at[j, u, p], g, partner(u // 2, p))

    def wide_tile(k):
        n = lax.rem(k, 2) * half_tiles + k // 2
        return tile(n), lax.rem(k, 2), n

    def lead_tile(h):
        return pl.ds(h * (features - lead), lead), h, tiles + h

    def r_copy(j, of, p):
        cols, h, n = of
        return remote(rows.at[j, piece(p), cols], back.at[j, piece(p), cols],
                      r_send.at[j, n, p], r_recv.at[j, n, p], g, partner(h, p))

    def e_copy(j, of):
        cols, h, n = of
        landing = lead_parts.at[h] if isinstance(h, int) else parts.at[j, :, packed(n)]
        return remote(block.at[j, near, cols], landing,
                      e_send.at[j, n], e_recv.at[j, n], g, first(h))

    def p_copy(j, n):
        return remote(block.at[j, own, tile(n)], chain.at[j - 1, :, packed(n)],
                      p_send.at[j, n], p_recv.at[j, n], before_me, me)

    def q_copy(j, h):
        return remote(block.at[j, pair, lead_tile(h)[0]], lead_chain.at[j - 1, h],
                      p_send.at[j, tiles + h], p_recv.at[j, tiles + h], before_me, me)

    loads = [
        pltpu.make_async_copy(tokens, block.at[0, own], load_sem.at[0]),
        pltpu.make_async_copy(gate_w, gate, load_sem.at[1]),
        pltpu.make_async_copy(up_w, up, load_sem.at[2]),
        pltpu.make_async_copy(down_w, down, load_sem.at[3]),
    ]
    loads[0].start()
    barrier = pltpu.get_barrier_semaphore()
    peers = [(g, partner(h, p)) for h in range(2) for p in (1, 2, 3) if (h, p) != (1, 1)]
    peers += [(group_at(1), me), (before_me, me)]
    for peer in peers:
        pl.semaphore_signal(barrier, inc=1, device_id=peer, device_id_type=MESH)

    def iota(shape, axis):
        return lax.broadcasted_iota(jnp.int32, shape, axis)

    member = jnp.zeros((experts, count), f32)
    weight = jnp.zeros((experts, count), f32)
    for k in range(ids.shape[0]):
        named = ids[k : k + 1, :] == iota((experts, count), 0)
        member = member + jnp.where(named, 1.0, 0.0)
        weight = weight + jnp.where(named, combine[k : k + 1, :], 0.0)
    before = jnp.where(iota((count, count), 0) < iota((count, count), 1), 1.0, 0.0).astype(bf16)
    rank = jnp.dot(member.astype(bf16), before, preferred_element_type=f32)
    slot = jnp.where(member > 0, rank, -1.0 - capacity)
    for q in range(groups):
        tables[0, q, 0:members] = slot[q * members : (q + 1) * members]
        tables[0, q, members : 2 * members] = weight[q * members : (q + 1) * members]

    pl.semaphore_wait(barrier, len(peers))
    loads[0].wait()

    def slots_of(j, h):
        lanes = []
        for p in range(4):
            e = partner(h, p)
            near_slot = near_tables[j, h, pl.ds(e, 1), :] + float(capacity)
            lanes.append(jnp.concatenate([tables[j, g, pl.ds(e, 1), :], near_slot], axis=1))
        return lanes

    def weights_of(j, h):
        lanes = []
        for p in range(4):
            e = members + partner(h, p)
            lanes.append(jnp.concatenate(
                [tables[j, g, pl.ds(e, 1), :], near_tables[j, h, pl.ds(e, 1), :]], axis=1))
        return lanes

    def places():
        return iota((piece_rows, 2 * count), 0).astype(f32)

    def begin(j):
        @pl.when(j >= 1)
        def _():
            t_copy(j).wait()

        for h in range(2):
            n_copy(j, h).start()

        @pl.when(j + 1 < groups)
        def _():
            t_copy(j + 1).start()

        @pl.when(j == 0)
        def _():
            for u in (0, 3):
                a_copy(j, u).start()

        for u in (1, 2):
            @pl.when(j >= 1)
            def _():
                z_copy(j, u).wait()

            a_copy(j, u).start()

            @pl.when(j + 1 < groups)
            def _():
                z_copy(j + 1, u).start()

        @pl.when(j == 0)
        def _():
            for load in loads[1:]:
                load.start()

    def pick(j, u):
        h = u // 2

        def choose(cols):
            chosen = jnp.dot(
                picks[h], block[j, :, cols], preferred_element_type=f32).astype(bf16)
            rows[j, 0:piece_rows, cols] = chosen[0:piece_rows]
            sending[lax.min(j, 1), :, cols] = chosen[piece_rows:width]

        if u in (1, 2):
            @pl.loop(h * half_picks, (h + 1) * half_picks)
            def _(n):
                choose(pl.ds(pl.multiple_of(ahead + n * pick_wide, 128), pick_wide))
        else:
            choose(span(u))
        for p in (2, 3, 1):
            x_copy(j, u, p).start()

    def prepare(j):
        for h in range(2):
            n_copy(j, h).wait()
            picks[h] = jnp.concatenate(
                [jnp.where(slot == places(), 1.0, 0.0) for slot in slots_of(j, h)], axis=0
            ).astype(bf16)

    def dispatch(j):
        for u in (1, 2):
            a_copy(j, u).wait()
            pick(j, u)

    def leads(j):
        for u in (0, 3):
            @pl.when(j == 0)
            def _():
                a_copy(j, u).wait()

            @pl.when(j >= 1)
            def _():
                z_copy(j, u).wait()

            @pl.when(j + 1 < groups)
            def _():
                z_copy(j + 1, u).start()
        for u in (0, 3):
            pick(j, u)

    def swapped(v):
        groups_of = [v[k * capacity : (k + 1) * capacity] for k in range(8)]
        return jnp.concatenate(
            [groups_of[4 * k + 2 * c + s] for s in range(2) for c in range(2) for k in range(2)], axis=0)

    def compute(j):
        @pl.when(j == 1)
        def _():
            loads[1].wait()
            loads[2].wait()
            loads[3].wait()

        for u in range(4):
            for p in (1, 2, 3):
                x_copy(j, u, p).wait()

        units = hidden.shape[2]

        @pl.loop(0, units // 256)
        def _(n):
            cols = pl.ds(pl.multiple_of(n * 256, 256), 256)

            def project(bank):
                left = jnp.dot(rows[j, :, 0:half], bank[0:half, cols], preferred_element_type=f32)
                right = jnp.dot(rows[j, :, half:features], bank[half:features, cols],
                                preferred_element_type=f32)
                return left + swapped(right)

            a = project(gate)
            b = project(up)
            value = jax.nn.silu(a) * b
            hidden[0, :, cols] = value.astype(bf16)
            hidden[1, :, cols] = swapped(value).astype(bf16)

        def project_back(of):
            cols, h, _ = of
            result = jnp.dot(hidden[h], down[:, cols], preferred_element_type=f32).astype(bf16)
            back[j, 0:piece_rows, cols] = result[0:piece_rows]
            rows[j, piece_rows:width, cols] = result[piece_rows:width]
            @pl.when(j >= 1)
            def _():
                send_back(j, of)

        for h in range(2):
            project_back(lead_tile(h))

        @pl.loop(0, tiles)
        def _(n):
            project_back(wide_tile(n))

    def send_back(j, of):
        for p in (2, 3, 1):
            r_copy(j, of, p).start()

    def send_all(j):
        @pl.loop(0, tiles)
        def _(n):
            send_back(j, wide_tile(n))

        for h in range(2):
            send_back(j, lead_tile(h))

    def gather(j, last):
        unit = jnp.where(iota((2 * count, 2 * count), 0) == iota((2 * count, 2 * count), 1), 1.0, 0.0).astype(bf16)
        for h in range(2):
            weights = jnp.concatenate(
                [jnp.where(slot == places(), weight, 0.0)
                 for slot, weight in zip(slots_of(j, h), weights_of(j, h))], axis=0)
            mix[h] = lax.dot_general(
                unit, weights.astype(bf16), (((1,), (1,)), ((), ())),
                preferred_element_type=f32).astype(bf16)

        def mixed(of):
            cols, h, _ = of
            for p in (1, 2, 3):
                r_copy(j, of, p).wait()
            return jnp.dot(mix[h], back[j, :, cols], preferred_element_type=f32)

        def blend_lead(h):
            of = lead_tile(h)
            both = mixed(of)
            if last:
                q_copy(groups - 1, h).wait()
                both = both + lead_chain[groups - 2, h].astype(f32)
                block[j, near, of[0]] = both[count : 2 * count].astype(bf16)
                e_copy(j, of).start()
                total[:, of[0]] = both[0:count]
            else:
                @pl.when(j == 1)
                def _():
                    block[j, :, of[0]] = both.astype(bf16)

                @pl.when(j >= 2)
                def _():
                    q_copy(j - 1, h).wait()
                    block[j, :, of[0]] = (both + lead_chain[j - 2, h].astype(f32)).astype(bf16)

                q_copy(j, h).start()

        def blend(k):
            of = wide_tile(k)
            both = mixed(of)
            block[j, near, of[0]] = both[count : 2 * count].astype(bf16)
            e_copy(j, of).start()
            total[:, of[0]] = both[0:count]
            if not last:
                @pl.when(j == groups - 1)
                def _():
                    send_back(0, of)

        if not last:
            for h in range(2):
                blend_lead(h)
        pl.loop(0, tiles)(blend)
        if not last:
            @pl.when(j == groups - 1)
            def _():
                for h in range(2):
                    send_back(0, lead_tile(h))
        if last:
            for h in range(2):
                blend_lead(h)

    def arrived(j, n):
        return chain[j, :, packed(n)].astype(f32)

    def finish(j):
        @pl.loop(0, tiles)
        def _(k):
            n = wide_tile(k)[2]
            e_copy(j, wide_tile(k)).wait()
            part = total[:, tile(n)] + parts[j, :, packed(n)].astype(f32)

            @pl.when(j == 1)
            def _():
                block[j, own, tile(n)] = part.astype(bf16)

            @pl.when(j >= 2)
            def _():
                p_copy(j - 1, n).wait()
                block[j, own, tile(n)] = (part + arrived(j - 2, n)).astype(bf16)

            p_copy(j, n).start()

    plan = (
        ("begin", 0), ("prepare", 0), ("leads", 0), ("dispatch", 0), ("begin", 1), ("prepare", 1),
        ("dispatch", 1), ("leads", 1), ("begin", 2), ("compute", 1), ("prepare", 2), ("dispatch", 2),
        ("leads", 2), ("compute", 0), ("begin", 3), ("gather", 1), ("compute", 2), ("prepare", 3),
        ("dispatch", 3), ("finish", 1), ("leads", 3), ("gather", 2), ("compute", 3), ("finish", 2),
        ("gather", 3), ("finish", 3),
    )
    acts = {"begin": begin, "prepare": prepare, "dispatch": dispatch, "leads": leads, "compute": compute,
            "gather": lambda j: gather(j, False), "finish": finish, "send": send_all}

    @pl.loop(0, len(plan))
    def _(step):
        for name, act in acts.items():
            at_steps = [(k, j) for k, (other, j) in enumerate(plan) if other == name]
            if not at_steps:
                continue
            now, which = False, 0
            for k, j in at_steps:
                now = (step == k) | now
                which = which + jnp.where(step == k, j, 0)

            @pl.when(now)
            def _(act=act, which=which):
                act(which)

    gather(0, True)

    def out_copy(of):
        return pltpu.make_async_copy(block.at[0, own, of[0]], out.at[:, of[0]], out_sem.at[of[2]])

    @pl.loop(0, tiles)
    def _(k):
        of = wide_tile(k)
        e_copy(0, of).wait()
        p_copy(groups - 1, of[2]).wait()
        block[0, own, of[0]] = (
            total[:, of[0]] + parts[0, :, packed(of[2])].astype(f32) + arrived(groups - 2, of[2])).astype(bf16)
        out_copy(of).start()

    for h in range(2):
        of = lead_tile(h)
        e_copy(0, of).wait()
        block[0, own, of[0]] = (total[:, of[0]] + lead_parts[h].astype(f32)).astype(bf16)
        out_copy(of).start()

    for h in range(2):
        out_copy(lead_tile(h)).wait()

    @pl.loop(0, tiles)
    def _(k):
        out_copy(wide_tile(k)).wait()


def fused(tokens, expert_ids, combine, gate_w, up_w, down_w):
    count, features = tokens.shape
    units = gate_w.shape[2]
    groups = lax.axis_size("group")
    members = lax.axis_size("local")
    experts = groups * members
    capacity = max(2, count * expert_ids.shape[1] * 5 // (4 * experts))
    if (groups, members) != (4, 8) or capacity % 8 or features % 2048 or units % 256 or count % 128:
        return plain(tokens, expert_ids, combine, gate_w, up_w, down_w)
    width = members * capacity
    lead = 768
    slots = 2 * ((features // 2 - lead) // 640) + 2
    half = jnp.bfloat16
    dma = pltpu.SemaphoreType.DMA
    anywhere = pl.BlockSpec(memory_space=pl.ANY)
    inside = pl.BlockSpec(memory_space=pltpu.VMEM)
    return pl.pallas_call(
        functools.partial(layer, capacity, 640, lead),
        out_shape=jax.ShapeDtypeStruct((count, features), half),
        in_specs=[inside, inside, anywhere, anywhere, anywhere, anywhere],
        out_specs=anywhere,
        scratch_shapes=[
            pltpu.VMEM((groups, 2 * count, features), half),
            pltpu.VMEM((groups, groups, 2 * members, count), jnp.float32),
            pltpu.VMEM((groups, 2, 2 * members, count), jnp.float32),
            pltpu.VMEM((2, width, 2 * count), half),
            pltpu.VMEM((2, width * 3 // 4, features), half),
            pltpu.VMEM((groups, width, features), half),
            pltpu.VMEM((groups, width, features), half),
            pltpu.VMEM((features, units), half),
            pltpu.VMEM((features, units), half),
            pltpu.VMEM((units, features), half),
            pltpu.VMEM((2, width, units), half),
            pltpu.VMEM((2, 2 * count, width), half),
            pltpu.VMEM((groups, count, features - 2 * lead), half),
            pltpu.VMEM((2, count, lead), half),
            pltpu.VMEM((groups - 1, count, features - 2 * lead), half),
            pltpu.VMEM((groups - 1, 2, 2 * count, lead), half),
            pltpu.VMEM((count, features), jnp.float32),
            dma((4,)), dma((slots,)),
            dma((groups,)), dma((groups,)),
            dma((groups, 2)), dma((groups, 2)),
            dma((groups, 4)), dma((groups, 4)),
            dma((groups, 4)), dma((groups, 4)),
            dma((groups, 4, 4)), dma((groups, 4, 4)),
            dma((groups, slots, 4)), dma((groups, slots, 4)),
            dma((groups, slots)), dma((groups, slots)),
            dma((groups, slots)), dma((groups, slots)),
        ],
        compiler_params=pltpu.CompilerParams(
            collective_id=0, has_side_effects=True, vmem_limit_bytes=63 * 1024 * 1024),
    )(expert_ids.T, combine.T, tokens, gate_w[0], up_w[0], down_w[0])


def solution(mesh):
    rows = P(("group", "local"), None)
    banks = P(("group", "local"), None, None)
    return jax.shard_map(
        fused,
        mesh=mesh,
        in_specs=(rows, rows, rows, banks, banks, banks),
        out_specs=rows,
        check_vma=False,
    )
```
